256 devices in a mesh: lat: 16 (over x_lo, y, core), lon: 16 (over z, x_hi).
Axes of the slice: x: 4 (x_hi: 2, x_lo: 2; x = x_hi * 2 + x_lo), y: 4, z: 8, core: 2. Of those that a mesh axis runs over, the one named last changes fastest.
Arguments:
- velocity: float32 [2, 20, 1024, 4096], P(None, None, 'lat', 'lon'), may hold values from -6 to 6
- tracer: float32 [2, 20, 1024, 4096], P(None, None, 'lat', 'lon'), may hold values from -6 to 6
- surface: float32 [1024, 4096], P('lat', 'lon'), may hold values from -6 to 6
- damping: float32 [1024, 4096], P('lat', 'lon'), may hold values from 0.01 to 1
- ocean: int32 [1024, 4096], P('lat', 'lon'), may hold values 0 or 1
Outputs:
- velocity_next: float32 [2, 20, 1024, 4096], P(None, None, 'lat', 'lon')
- tracer_next: float32 [2, 20, 1024, 4096], P(None, None, 'lat', 'lon')
- surface_next: float32 [1024, 4096], P('lat', 'lon')
The draws below stay inside these ranges and needn't reach their ends.
Inputs may be any that keep to these rules, and one draw needn't show every extreme that they name: 1 marks an ocean cell, 0 a land cell.
All inputs are finite; a program needn't handle non-finite values. No bound on the sum of `ocean` on one device may be relied on, other than what follows from the above.
Results may differ from the reference program's by a relative error of at most 0.000024.
Values sent between devices are 32-bit elements; how exact they have to be, the bound alone decides.
A program may use at most 64 MiB of HBM per device.

```python
import math
import jax
import jax.numpy as jnp
from jax import lax

LEVELS = 20
TRACERS = 2
SWEEPS = 8
NY = 1024
NX = 4096


def with_ends(drawn, own_key, least, high):
    extent = drawn.shape
    spot = [jax.random.randint(jax.random.fold_in(own_key, axis), (), 0, extent[axis]) for axis in range(len(extent))]
    drawn = drawn.at[tuple(spot)].set(least)
    longest = extent.index(max(extent))
    spot[longest] = (spot[longest] + 1) % extent[longest]
    return drawn.at[tuple(spot)].set(high)


def block_levels(rng, extent, shards, least, high):
    def one(position, blocks):
        heights = jax.random.uniform(jax.random.fold_in(jax.random.fold_in(rng, 6), position), (blocks,), jnp.float32, least / len(shards), high / len(shards))
        return jnp.repeat(jnp.exp(heights), extent[position] // blocks).reshape((-1,) + (1,) * (len(extent) - position - 1))

    level = one(*shards[0])
    for cut in shards[1:]:
        level = level * one(*cut)
    return level


def gaussian(key, extent, width, limit, shards=(), kind=jnp.bfloat16):
    entries = width * jax.random.normal(key, extent, jnp.float32)
    if shards:
        entries = entries * block_levels(key, extent, shards, -0.22, 0.18)
    return jnp.clip(entries, -limit, limit).astype(kind)


def setup_inputs(seed: int = 0) -> dict:
    key_list = jax.random.split(jax.random.key(seed), 6)
    velocity = gaussian(key_list[0], (2, LEVELS, NY, NX), 1.0, 6.0, ((2, 16), (3, 16)), jnp.float32)
    tracer = gaussian(key_list[1], (TRACERS, LEVELS, NY, NX), 1.0, 6.0, ((2, 16), (3, 16)), jnp.float32)
    surface = gaussian(key_list[2], (NY, NX), 1.0, 6.0, ((0, 16), (1, 16)), jnp.float32)
    damping = jnp.clip(jnp.exp(math.log(1.0) - 4.6051702 * jax.random.uniform(key_list[3], (NY, NX), jnp.float32) ** block_levels(key_list[3], (NY, NX), ((0, 16), (1, 16)), -0.2, 0.2)), 0.01, 1.0)
    ocean = with_ends((jax.random.randint(key_list[4], (NY, NX), 0, 5) < 4).astype(jnp.int32), jax.random.fold_in(key_list[4], 1), 0, 1)
    return {"velocity": velocity, "tracer": tracer, "surface": surface, "damping": damping, "ocean": ocean}


time_step = 0.2
gravity = 4.0
coriolis = 1.0
viscosity = 0.5
diffusivity = 0.5
thermal = 0.2
haline = 0.15
buoyancy = 2.0
transport = 1.0
damping_floor = 0.01


def sweep_weights(count):
    low = damping_floor / (damping_floor + 4.0)
    high = 2.0 - low
    theta = (high + low) / 2.0
    delta = (high - low) / 2.0
    sigma = theta / delta
    weights = [(0.0, 1.0 / theta)]
    rho_now = 1.0 / sigma
    for _ in range(count - 1):
        rho_new = 1.0 / (2.0 * sigma - rho_now)
        weights.append((rho_new * rho_now, 2.0 * rho_new / delta))
        rho_now = rho_new
    return weights


def shifts(field):
    east = jnp.roll(field, -1, axis=-1)
    west = jnp.roll(field, 1, axis=-1)
    zero_row = jnp.zeros_like(field[..., :1, :])
    north = jnp.concatenate([field[..., 1:, :], zero_row], axis=-2)
    south = jnp.concatenate([zero_row, field[..., :-1, :]], axis=-2)
    return (field, east, west, north, south)


def laplace(parts, faces):
    centre, east, west, north, south = parts
    face_e, face_w, face_n, face_s = faces
    return face_e * (east - centre) + face_w * (west - centre) + face_n * (north - centre) + face_s * (south - centre)


def slope_x(parts, faces):
    centre, east, west, north, south = parts
    return (faces[0] * (east - centre) + faces[1] * (centre - west)) * 0.5


def slope_y(parts, faces):
    centre, east, west, north, south = parts
    return (faces[2] * (north - centre) + faces[3] * (centre - south)) * 0.5


def spread(u_parts, v_parts, faces):
    part_x = (faces[0] * (u_parts[1] + u_parts[0]) - faces[1] * (u_parts[0] + u_parts[2])) * 0.5
    part_y = (faces[2] * (v_parts[3] + v_parts[0]) - faces[3] * (v_parts[0] + v_parts[4])) * 0.5
    return part_x + part_y


def reference(velocity, tracer, surface, damping, ocean):
    mask = ocean.astype(jnp.float32)
    mask_parts = shifts(mask)
    faces = (mask * mask_parts[1], mask * mask_parts[2], mask * mask_parts[3], mask * mask_parts[4])
    rows = jnp.arange(NY).astype(jnp.float32)
    planet = (coriolis * (2.0 * (rows + 0.5) / NY - 1.0))[:, None]
    levels = jnp.arange(LEVELS).astype(jnp.float32)
    thick = 2.0 * (levels + 1.0) / (LEVELS * (LEVELS + 1))

    def level_step(carry, items):
        press_prev, column = carry
        u_now, v_now, temp, salt, dz_k = items
        pressure = press_prev + buoyancy * (dz_k * (thermal * temp - haline * salt))
        up = shifts(u_now)
        vp = shifts(v_now)
        pp = shifts(pressure)
        star_u = u_now + time_step * (planet * v_now - slope_x(pp, faces) + viscosity * laplace(up, faces))
        star_v = v_now + time_step * (-planet * u_now - slope_y(pp, faces) + viscosity * laplace(vp, faces))
        news = []
        for field in (temp, salt):
            tp = shifts(field)
            tend = diffusivity * laplace(tp, faces) - u_now * slope_x(tp, faces) - v_now * slope_y(tp, faces)
            news.append(field + time_step * mask * tend)
        column = column + dz_k * spread(up, vp, faces)
        return (pressure, column), (star_u, star_v, news[0], news[1])

    zero = jnp.zeros((NY, NX), jnp.float32)
    (press_last, column), (star_u, star_v, temp_new, salt_new) = lax.scan(
        level_step, (zero, zero), (velocity[0], velocity[1], tracer[0], tracer[1], thick))
    forcing = damping * surface - transport * column
    diag = damping + faces[0] + faces[1] + faces[2] + faces[3]
    state = surface
    step_dir = jnp.zeros_like(surface)
    for weight_a, weight_c in sweep_weights(SWEEPS):
        centre, east, west, north, south = shifts(state)
        applied = diag * centre - faces[0] * east - faces[1] * west - faces[2] * north - faces[3] * south
        resid = forcing - applied
        step_dir = weight_a * step_dir + weight_c * (resid / diag)
        state = state + step_dir
    sp = shifts(state)
    u_next = mask * (star_u - time_step * gravity * slope_x(sp, faces))
    v_next = mask * (star_v - time_step * gravity * slope_y(sp, faces))
    return jnp.stack([u_next, v_next]), jnp.stack([temp_new, salt_new]), state
```

```python
import functools

import jax
import jax.numpy as jnp
from jax import lax
from jax.experimental import pallas as pl
from jax.experimental.pallas import tpu as pltpu
from jax.sharding import PartitionSpec as P

SWEEPS = 8

time_step = 0.2
gravity = 4.0
coriolis = 1.0
viscosity = 0.5
diffusivity = 0.5
thermal = 0.2
haline = 0.15
buoyancy = 2.0
transport = 1.0
damping_floor = 0.01

LANES = 128
HALO = 9
TOP = 16
MESH = pl.DeviceIdType.MESH
SURF, MASK, DAMP, USUM, VSUM = range(5)


def sweep_weights(count):
    low = damping_floor / (damping_floor + 4.0)
    high = 2.0 - low
    theta = (high + low) / 2.0
    delta = (high - low) / 2.0
    sigma = theta / delta
    weights = [(0.0, 1.0 / theta)]
    rho_now = 1.0 / sigma
    for _ in range(count - 1):
        rho_new = 1.0 / (2.0 * sigma - rho_now)
        weights.append((rho_new * rho_now, 2.0 * rho_new / delta))
        rho_now = rho_new
    return weights


def lanes_of(rows):
    return lax.broadcasted_iota(jnp.int32, (rows, LANES), 1)


def shift(x, by):
    if isinstance(by, int):
        by %= LANES
        if by == 0:
            return x
    return pltpu.roll(x, by, 1)


def east_of(q, last):
    r = [shift(x, -1) for x in q]
    n = len(q)
    return [jnp.where(last, r[(i + 1) % n], r[i]) for i in range(n)]


def west_of(q, first):
    r = [shift(x, 1) for x in q]
    n = len(q)
    return [jnp.where(first, r[(i - 1) % n], r[i]) for i in range(n)]


def step_kernel(
    levels, rows, lat_n, lon_n,
    vel, tra, srf, dmp, ocn,
    vo, to, cuv, so,
    vb, tb, pb, oc, ext, xb, dd, co, cf,
    msg_e, msg_w, got_e, got_w, corner,
    msg_n, msg_s, got_n, got_s,
    col_e, col_w, gcol_e, gcol_w,
    row_n, row_s, grow_n, grow_s,
    local_sem, send_sem, recv_sem,
):
    L, R = levels, rows
    lat, lon = lax.axis_index("lat"), lax.axis_index("lon")
    north, south = lax.rem(lat + 1, lat_n), lax.rem(lat + lat_n - 1, lat_n)
    east, west = lax.rem(lon + 1, lon_n), lax.rem(lon + lon_n - 1, lon_n)

    barrier = pltpu.get_barrier_semaphore()
    peers = [(a, b) for a in (lat, north, south) for b in (lon, east, west)][1:]
    for peer in peers:
        pl.semaphore_signal(barrier, inc=1, device_id=peer, device_id_type=MESH)

    count = [0]

    def fetch(src, dst):
        copy = pltpu.make_async_copy(src, dst, local_sem.at[count[0]])
        count[0] += 1
        copy.start()
        return copy

    def half(h):
        return pl.ds(h * LANES, LANES)

    inner = pl.ds(TOP, R)
    small = []
    for h in range(2):
        small.append(fetch(ocn.at[:, half(h)], oc.at[h]))
        small.append(fetch(srf.at[:, half(h)], ext.at[SURF, h, inner]))
        small.append(fetch(dmp.at[:, half(h)], ext.at[DAMP, h, inner]))
    chunk = L // 2
    vel_copies, tra_copies = [], []
    for src, dst, copies in ((vel, vb, vel_copies), (tra, tb, tra_copies)):
        for c in range(2):
            for part in range(2):
                for h in range(2):
                    start = (c * L + part * chunk) * R
                    copies.append((c, part, h, fetch(
                        src.at[pl.ds(start, chunk * R), half(h)],
                        dst.at[h, pl.ds(8 + start, chunk * R)])))

    zero8 = jnp.zeros((8, LANES), jnp.float32)
    for h in range(2):
        for buf, size in ((vb, 2 * L * R), (tb, 2 * L * R), (pb, L * R)):
            buf[h, 0:8] = zero8
            buf[h, 8 + size:16 + size] = zero8

    for copy in small:
        copy.wait()
    for h in range(2):
        ext[MASK, h, TOP:TOP + R] = oc[h].astype(jnp.float32)

    mid = R // 2
    lane_m = lanes_of(mid)

    def pack_cols(field, acc_w, acc_e):
        off = HALO * field
        for part in range(2):
            at = off + 64 * part
            keep = (lane_m >= at) & (lane_m < at + HALO)
            rows_here = slice(TOP + mid * part, TOP + mid * (part + 1))
            acc_w = jnp.where(keep, shift(ext[field, 0, rows_here], at), acc_w)
            acc_e = jnp.where(keep, shift(ext[field, 1, rows_here], at + HALO), acc_e)
        return acc_w, acc_e

    def pack_rows(field):
        for h in range(2):
            msg_n[h, 8 * field:8 * field + 8] = ext[field, h, TOP + R - 8:TOP + R]
            msg_s[h, 8 * field:8 * field + 8] = ext[field, h, TOP:TOP + 8]

    far = ((SURF, 0), (MASK, 1), (VSUM, 2))

    def pack_far(field, place):
        for h in range(2):
            msg_n[h, 40 + place:41 + place] = ext[field, h, TOP + R - 9:TOP + R - 8]
            msg_s[h, 40 + place:41 + place] = ext[field, h, TOP + 8:TOP + 9]

    for h in range(2):
        msg_n[h, 40:48] = zero8
        msg_s[h, 40:48] = zero8
    accs = (jnp.zeros((mid, LANES), jnp.float32),) * 2
    for field in (SURF, MASK, DAMP):
        accs = pack_cols(field, *accs)
        pack_rows(field)
    pack_far(*far[0])
    pack_far(*far[1])
    msg_w[...], msg_e[...] = accs

    thick = [2.0 * (k + 1.0) / (L * (L + 1)) for k in range(L)]
    for c, part, h, copy in vel_copies:
        copy.wait()
        total = None if part == 0 else ext[USUM + c, h, TOP:TOP + R]
        for k in range(part * chunk, (part + 1) * chunk):
            at = 8 + (c * L + k) * R
            term = thick[k] * vb[h, at:at + R]
            total = term if total is None else total + term
        ext[USUM + c, h, TOP:TOP + R] = total
    accs = (msg_w[...], msg_e[...])
    for field in (USUM, VSUM):
        accs = pack_cols(field, *accs)
        pack_rows(field)
    pack_far(*far[2])
    msg_w[...], msg_e[...] = accs

    pl.semaphore_wait(barrier, 8)
    sent = []

    def send(src, dst, peer):
        i = len(sent)
        copy = pltpu.make_async_remote_copy(
            src_ref=src, dst_ref=dst, send_sem=send_sem.at[i], recv_sem=recv_sem.at[i],
            device_id=peer, device_id_type=MESH)
        copy.start()
        sent.append(copy)

    send(msg_e, got_w, (lat, east))
    send(msg_w, got_e, (lat, west))
    send(msg_e.at[pl.ds(mid - 8, 8)], corner.at[3], (north, east))
    send(msg_w.at[pl.ds(mid - 8, 8)], corner.at[2], (north, west))
    send(msg_e.at[pl.ds(0, 8)], corner.at[1], (south, east))
    send(msg_w.at[pl.ds(0, 8)], corner.at[0], (south, west))
    send(msg_n, got_s, (north, lon))
    send(msg_s, got_n, (south, lon))
    urgent = list(sent)

    scale = 0.5 * time_step
    lane_r = lanes_of(R)
    first_r, last_r = lane_r == 0, lane_r == LANES - 1
    row_r = lax.broadcasted_iota(jnp.int32, (R, LANES), 0)
    m = [ext[MASK, h, TOP:TOP + R] for h in range(2)]
    m_east, m_west = east_of(m, last_r), west_of(m, first_r)
    j = (row_r + lat * R).astype(jnp.float32)
    planet = coriolis * (2.0 * (j + 0.5) / (R * lat_n) - 1.0)
    for h in range(2):
        fe, fw = m[h] * m_east[h], m[h] * m_west[h]
        if h == 1:
            fe = jnp.where(last_r, 0.0, fe)
        else:
            fw = jnp.where(first_r, 0.0, fw)
        fn = jnp.where(row_r == R - 1, 0.0, m[h] * pltpu.roll(m[h], R - 1, 0))
        fs = jnp.where(row_r == 0, 0.0, m[h] * pltpu.roll(m[h], 1, 0))
        for i, value in enumerate((scale * fe, scale * fw, scale * fn, scale * fs, m[h],
                                   time_step * planet * m[h])):
            cf[i, h] = value

    for *_, copy in tra_copies:
        copy.wait()
    for h in range(2):
        press = None
        for k in range(L):
            at = 8 + k * R
            warm = (buoyancy * thermal * thick[k]) * tb[h, at:at + R]
            salt = (buoyancy * haline * thick[k]) * tb[h, at + L * R:at + L * R + R]
            press = warm - salt if press is None else press + (warm - salt)
            pb[h, at:at + R] = press

    stacks = ((vb, 0), (vb, 1), (tb, 0), (tb, 1), (pb, 0))

    def pack_level(k, accs):
        acc_w, acc_e = accs
        for f, (buf, c) in enumerate(stacks):
            at = pl.multiple_of(8 + (c * L + k) * R, 8)
            lane = f * L + k
            keep = lane_r == lane
            acc_w = jnp.where(keep, shift(buf[0, pl.ds(at, R)], lane), acc_w)
            acc_e = jnp.where(keep, shift(buf[1, pl.ds(at, R)], lane + 1), acc_e)
        return acc_w, acc_e

    zero_r = jnp.zeros((R, LANES), jnp.float32)
    col_w[...], col_e[...] = lax.fori_loop(0, L, pack_level, (zero_r, zero_r))
    for h in range(2):
        for out, row in ((row_n, R - 1), (row_s, 0)):
            out[h, 5 * L // 8 * 8:] = zero8
            for buf, base, n in ((vb, 0, 2 * L), (tb, 2 * L, 2 * L), (pb, 4 * L, L)):
                for k in range(0, n, 8):
                    size = min(8, n - k)
                    out[h, base + k:base + k + size] = buf[h, pl.ds(8 + row + k * R, size, stride=R)]
    send(col_e, gcol_w, (lat, east))
    send(col_w, gcol_e, (lat, west))
    send(row_n, grow_s, (north, lon))
    send(row_s, grow_n, (south, lon))
    late = sent[len(urgent):]

    lane_8 = lanes_of(8)
    first, last = lane_8 == 0, lane_8 == LANES - 1

    def level(k, carry):
        at_u = pl.multiple_of(k * R, R)
        at_v = pl.multiple_of((L + k) * R, R)

        def views(buf, at):
            return [buf.at[h, pl.ds(at, R + 16)] for h in range(2)]

        uv, vv = views(vb, at_u), views(vb, at_v)
        tv, sv = views(tb, at_u), views(tb, at_v)
        pv = views(pb, at_u)
        for r in range(0, R, 8):
            def get(view, by=0):
                return [view[h][8 + r + by:16 + r + by] for h in range(2)]

            fe, fw, fn, fs, ms, fc = [[cf[i, h, r:r + 8] for h in range(2)] for i in range(6)]
            u, v, p = get(uv), get(vv), get(pv)
            up = [1.0 + x for x in u]
            um = [1.0 - x for x in u]
            vp = [1.0 + x for x in v]
            vm = [1.0 - x for x in v]
            for view, at in ((tv, at_u), (sv, at_v)):
                q, qn, qs = get(view), get(view, 1), get(view, -1)
                qe = east_of(q, last)
                gx = [fe[h] * (qe[h] - q[h]) for h in range(2)]
                gw = west_of(gx, first)
                for h in range(2):
                    gn = fn[h] * (qn[h] - q[h])
                    gs = fs[h] * (q[h] - qs[h])
                    to[h, pl.ds(at + r, 8)] = (
                        q[h] + (gx[h] * um[h] - gw[h] * up[h]) + (gn * vm[h] - gs * vp[h]))
            un, us = get(uv, 1), get(uv, -1)
            less = [u[h] - p[h] for h in range(2)]
            more = [u[h] + p[h] for h in range(2)]
            less_e, more_w = east_of(less, last), west_of(more, first)
            for h in range(2):
                along = fe[h] * (less_e[h] - less[h]) - fw[h] * (more[h] - more_w[h])
                across = fn[h] * (un[h] - u[h]) - fs[h] * (u[h] - us[h])
                vo[h, pl.ds(at_u + r, 8)] = (ms[h] * u[h] + fc[h] * v[h]) + (along + across)
            vn, vs, pn, ps = get(vv, 1), get(vv, -1), get(pv, 1), get(pv, -1)
            ve = east_of(v, last)
            gx = [fe[h] * (ve[h] - v[h]) for h in range(2)]
            gw = west_of(gx, first)
            for h in range(2):
                across = (fn[h] * ((vn[h] - pn[h]) - (v[h] - p[h]))
                          - fs[h] * ((v[h] + p[h]) - (vs[h] + ps[h])))
                vo[h, pl.ds(at_v + r, 8)] = (ms[h] * v[h] - fc[h] * u[h]) + ((gx[h] - gw[h]) + across)
        return carry

    lax.fori_loop(0, L, level, 0)

    for copy in urgent:
        copy.wait_recv()
    keep_s = jnp.where(lat == 0, 0.0, 1.0)
    keep_n = jnp.where(lat == lat_n - 1, 0.0, 1.0)
    low, high = TOP - 8, TOP + R
    low_m, low_8 = lane_m < 64, lane_8 < 64
    for f in range(5):
        off = HALO * f
        ks, kn = (keep_s, keep_n) if f == MASK else (1.0, 1.0)
        for h in range(2):
            ext[f, h, low:low + 8] = got_s[h, 8 * f:8 * f + 8] * ks
            ext[f, h, high:high + 8] = got_n[h, 8 * f:8 * f + 8] * kn
        for part in range(2):
            at = off + 64 * part
            ext[f, 2, TOP + mid * part:TOP + mid * (part + 1)] = jnp.where(
                low_m, shift(got_e[...], -at), shift(got_w[...], LANES - HALO - at))
        ext[f, 2, high:high + 8] = kn * jnp.where(
            low_8, shift(corner[0], -off), shift(corner[1], LANES - HALO - off))
        ext[f, 2, low:low + 8] = ks * jnp.where(
            low_8, shift(corner[2], -off - 64), shift(corner[3], LANES - HALO - off - 64))
    for f, place in far:
        ks, kn = (keep_s, keep_n) if f == MASK else (1.0, 1.0)
        for h in range(2):
            ext[f, h, low - 1:low] = got_s[h, 40 + place:41 + place] * ks
            ext[f, h, high + 8:high + 9] = got_n[h, 40 + place:41 + place] * kn

    step = 16
    lane_s = lanes_of(step)
    first_s, last_s = lane_s == 0, lane_s == LANES - 1
    for r in range(0, R + 16, step):
        def near(f, by=0):
            return [ext[f, t, low + r + by:low + r + by + step] for t in range(3)]

        mm, mn, msth = near(MASK), near(MASK, 1), near(MASK, -1)
        me, mw = east_of(mm, last_s), west_of(mm, first_s)
        us, vs, vn, vso = near(USUM), near(VSUM), near(VSUM, 1), near(VSUM, -1)
        ue, uw = east_of(us, last_s), west_of(us, first_s)
        ss, ds = near(SURF), near(DAMP)
        for t in range(3):
            fe, fw, fn, fs = mm[t] * me[t], mm[t] * mw[t], mm[t] * mn[t], mm[t] * msth[t]
            column = 0.5 * ((fe * (ue[t] + us[t]) - fw * (us[t] + uw[t]))
                            + (fn * (vn[t] + vs[t]) - fs * (vs[t] + vso[t])))
            forcing = ds[t] * ss[t] - transport * column
            inv = 1.0 / (ds[t] + fe + fw + fn + fs)
            for i, value in enumerate((forcing, fe, fw, fn, fs)):
                co[i, t, r:r + step] = value * inv

    for n, (wa, wc) in enumerate(sweep_weights(SWEEPS)):
        def rd(t, at, n=n):
            return ext[SURF, t, at:at + step] if n % 2 == 0 else xb[t, at:at + step]

        for r in range(0, R + 16, step):
            at = low + r
            x = [rd(t, at) for t in range(3)]
            xe, xw = east_of(x, last_s), west_of(x, first_s)
            for t in range(3):
                g, ce, cw, cn, cs = [co[i, t, r:r + step] for i in range(5)]
                resid = (((g - x[t]) + ce * xe[t]) + (cw * xw[t] + cn * rd(t, at + 1))) + cs * rd(t, at - 1)
                move = wc * resid
                if n > 0:
                    move = move + wa * dd[t, r:r + step]
                dd[t, r:r + step] = move
                if n % 2 == 0:
                    xb[t, at:at + step] = x[t] + move
                else:
                    ext[SURF, t, at:at + step] = x[t] + move

    push = 0.5 * time_step * gravity
    for r in range(0, R, step):
        def near(f, by=0):
            return [ext[f, t, TOP + r + by:TOP + r + by + step] for t in range(3)]

        mm, mn, msth = near(MASK), near(MASK, 1), near(MASK, -1)
        me, mw = east_of(mm, last_s), west_of(mm, first_s)
        x, xn, xs = near(SURF), near(SURF, 1), near(SURF, -1)
        xe, xw = east_of(x, last_s), west_of(x, first_s)
        for h in range(2):
            k = push * mm[h]
            cuv[0, h, r:r + step] = k * (me[h] * (xe[h] - x[h]) + mw[h] * (x[h] - xw[h]))
            cuv[1, h, r:r + step] = k * (mn[h] * (xn[h] - x[h]) + msth[h] * (x[h] - xs[h]))
            so[h, r:r + step] = x[h]

    for copy in late:
        copy.wait_recv()
    mask_e = ext[MASK, 1, TOP:TOP + R][:, LANES - 1:] * ext[MASK, 2, TOP:TOP + R][:, :1]
    mask_w = ext[MASK, 0, TOP:TOP + R][:, :1] * ext[MASK, 2, TOP:TOP + R][:, LANES - 1:]
    own_e, own_w = col_e[...], col_w[...]
    g_e = (scale * mask_e) * (gcol_e[...] - own_e)
    g_w = (scale * mask_w) * (own_w - gcol_w[...])

    def beside(own):
        return jnp.where(lane_r < 3 * L, shift(own, 2 * L), shift(own, 3 * L))

    def choose(u_part, v_part, t_part):
        return jnp.where(lane_r < L, u_part, jnp.where(lane_r < 2 * L, v_part, t_part))

    fix_e = choose(g_e - shift(g_e, -4 * L), g_e, g_e * (1.0 - beside(own_e)))
    fix_w = -choose(g_w + shift(g_w, -4 * L), g_w, g_w * (1.0 + beside(own_w)))

    def unpack(k, carry):
        for f in range(4):
            out, c = (vo, f) if f < 2 else (to, f - 2)
            lane = f * L + k
            at = pl.multiple_of((c * L + k) * R, R)
            out[0, pl.ds(at, R)] += jnp.where(first_r, shift(fix_w, LANES - lane), 0.0)
            out[1, pl.ds(at, R)] += jnp.where(last_r, shift(fix_e, LANES - 1 - lane), 0.0)
        return carry

    lax.fori_loop(0, L, unpack, 0)
    for h in range(2):
        mask_n = scale * ext[MASK, h, TOP + R - 1:TOP + R] * ext[MASK, h, TOP + R:TOP + R + 1]
        mask_s = scale * ext[MASK, h, TOP:TOP + 1] * ext[MASK, h, TOP - 1:TOP]

        def parts(f):
            return slice(f * L, (f + 1) * L)

        gn = [mask_n * (grow_n[h, parts(f)] - row_n[h, parts(f)]) for f in range(5)]
        gs = [mask_s * (row_s[h, parts(f)] - grow_s[h, parts(f)]) for f in range(5)]
        vn, vs = row_n[h, parts(1)], row_s[h, parts(1)]
        fix_n = (gn[0], gn[1] - gn[4], gn[2] * (1.0 - vn), gn[3] * (1.0 - vn))
        fix_s = (-gs[0], -(gs[1] + gs[4]), -gs[2] * (1.0 + vs), -gs[3] * (1.0 + vs))
        for f in range(4):
            out, c = (vo, f) if f < 2 else (to, f - 2)
            for fix, row in ((fix_n[f], R - 1), (fix_s[f], 0)):
                for k in range(0, L, 8):
                    size = min(8, L - k)
                    at = pl.ds((c * L + k) * R + row, size, stride=R)
                    out[h, at] = out[h, at] + fix[k:k + size]

    for copy in sent:
        copy.wait_send()


def write_kernel(levels, rows, vo, to, cuv, so, vel_next, tra_next, srf_next, vbuf, sem):
    L, R = levels, rows
    copies = []

    def put(src, dst):
        copy = pltpu.make_async_copy(src, dst, sem.at[len(copies)])
        copy.start()
        copies.append(copy)

    def half(h):
        return pl.ds(h * LANES, LANES)

    for h in range(2):
        for c in range(2):
            here = pl.ds(c * L * R, L * R)
            put(to.at[h, here], tra_next.at[here, half(h)])
    for h in range(2):
        put(so.at[h], srf_next.at[:, half(h)])
    chunk = L // 2
    for c in range(2):
        for part in range(2):
            for h in range(2):
                shared = cuv[c, h]
                for k in range(part * chunk, (part + 1) * chunk):
                    at = (c * L + k) * R
                    vbuf[h, at:at + R] = vo[h, at:at + R] - shared
                here = pl.ds((c * L + part * chunk) * R, chunk * R)
                put(vbuf.at[h, here], vel_next.at[here, half(h)])
    for copy in copies:
        copy.wait()


def shards(lat_n, lon_n, velocity, tracer, surface, damping, ocean):
    _, L, R, C = velocity.shape
    f32 = jnp.float32
    anywhere = pl.BlockSpec(memory_space=pl.ANY)
    inside = pl.BlockSpec(memory_space=pltpu.VMEM)

    def scratch(*shape):
        return pltpu.VMEM(shape, f32)

    flat = 2 * L * R
    ring = R + 2 * TOP
    mid = [
        pltpu.VMEM((2, flat, LANES), f32),
        pltpu.VMEM((2, flat, LANES), f32),
        pltpu.VMEM((2, 2, R, LANES), f32),
        pltpu.VMEM((2, R, LANES), f32),
    ]
    packed = 5 * L // 8 * 8 + 8
    made = pl.pallas_call(
        functools.partial(step_kernel, L, R, lat_n, lon_n),
        out_shape=mid,
        in_specs=[anywhere] * 5,
        out_specs=[inside] * 4,
        scratch_shapes=[
            scratch(2, flat + 16, LANES), scratch(2, flat + 16, LANES), scratch(2, L * R + 16, LANES),
            pltpu.VMEM((2, R, LANES), jnp.int32),
            scratch(5, 3, ring, LANES), scratch(3, ring, LANES), scratch(3, R + 16, LANES),
            scratch(5, 3, R + 16, LANES), scratch(6, 2, R, LANES),
            scratch(R // 2, LANES), scratch(R // 2, LANES), scratch(R // 2, LANES), scratch(R // 2, LANES),
            scratch(4, 8, LANES),
            scratch(2, 48, LANES), scratch(2, 48, LANES), scratch(2, 48, LANES), scratch(2, 48, LANES),
            scratch(R, LANES), scratch(R, LANES), scratch(R, LANES), scratch(R, LANES),
            scratch(2, packed, LANES), scratch(2, packed, LANES),
            scratch(2, packed, LANES), scratch(2, packed, LANES),
            pltpu.SemaphoreType.DMA((22,)),
            pltpu.SemaphoreType.DMA((12,)),
            pltpu.SemaphoreType.DMA((12,)),
        ],
        compiler_params=pltpu.CompilerParams(
            collective_id=0, has_side_effects=True, vmem_limit_bytes=32 * 1024 * 1024),
        name="ocean_step",
    )(*[
        pltpu.with_memory_space_constraint(x, pltpu.HBM)
        for x in (velocity.reshape(flat, C), tracer.reshape(flat, C), surface, damping, ocean)
    ])
    vel_next, tra_next, srf_next = pl.pallas_call(
        functools.partial(write_kernel, L, R),
        out_shape=[
            jax.ShapeDtypeStruct((flat, C), f32),
            jax.ShapeDtypeStruct((flat, C), f32),
            jax.ShapeDtypeStruct((R, C), f32),
        ],
        in_specs=[inside] * 4,
        out_specs=[anywhere] * 3,
        scratch_shapes=[scratch(2, flat, LANES), pltpu.SemaphoreType.DMA((14,))],
        compiler_params=pltpu.CompilerParams(vmem_limit_bytes=32 * 1024 * 1024),
        name="ocean_write",
    )(*made)
    return vel_next.reshape(velocity.shape), tra_next.reshape(tracer.shape), srf_next


def solution(mesh):
    placed = (
        P(None, None, "lat", "lon"),
        P(None, None, "lat", "lon"),
        P("lat", "lon"),
        P("lat", "lon"),
        P("lat", "lon"),
    )
    return jax.shard_map(
        functools.partial(shards, mesh.shape["lat"], mesh.shape["lon"]),
        mesh=mesh,
        in_specs=placed,
        out_specs=(P(None, None, "lat", "lon"), P(None, None, "lat", "lon"), P("lat", "lon")),
        check_vma=False,
    )
```

```python
import functools

import jax
import jax.numpy as jnp
from jax import lax
from jax.experimental import pallas as pl
from jax.experimental.pallas import tpu as pltpu
from jax.sharding import PartitionSpec as P

SWEEPS = 8

time_step = 0.2
gravity = 4.0
coriolis = 1.0
viscosity = 0.5
diffusivity = 0.5
thermal = 0.2
haline = 0.15
buoyancy = 2.0
transport = 1.0
damping_floor = 0.01

LANES = 128
PIECES = 2
MEET = 10
HALO = 9
TOP = 16
MESH = pl.DeviceIdType.MESH
SURF, MASK, DAMP, USUM, VSUM = range(5)


def sweep_weights(count):
    low = damping_floor / (damping_floor + 4.0)
    high = 2.0 - low
    theta = (high + low) / 2.0
    delta = (high - low) / 2.0
    sigma = theta / delta
    weights = [(0.0, 1.0 / theta)]
    rho_now = 1.0 / sigma
    for _ in range(count - 1):
        rho_new = 1.0 / (2.0 * sigma - rho_now)
        weights.append((rho_new * rho_now, 2.0 * rho_new / delta))
        rho_now = rho_new
    return weights


def lanes_of(rows):
    return lax.broadcasted_iota(jnp.int32, (rows, LANES), 1)


def shift(x, by):
    if isinstance(by, int):
        by %= LANES
        if by == 0:
            return x
    return pltpu.roll(x, by, 1)


def east_of(q, last):
    r = [shift(x, -1) for x in q]
    n = len(q)
    return [jnp.where(last, r[(i + 1) % n], r[i]) for i in range(n)]


def west_of(q, first):
    r = [shift(x, 1) for x in q]
    n = len(q)
    return [jnp.where(first, r[(i - 1) % n], r[i]) for i in range(n)]


def step_kernel(
    levels, rows, lat_n, lon_n,
    vel, tra, srf, dmp, ocn,
    vo, to, cuv, so, fix,
    vb, tb, pb, oc, ext, xb, dd, co, cf,
    msg_e, msg_w, got_e, got_w, corner,
    msg_n, msg_s, got_n, got_s,
    col_e, col_w, gcol_e, gcol_w,
    row_n, row_s, grow_n, grow_s,
    local_sem, send_sem, recv_sem,
):
    L, R = levels, rows
    lat, lon = lax.axis_index("lat"), lax.axis_index("lon")
    north, south = lax.rem(lat + 1, lat_n), lax.rem(lat + lat_n - 1, lat_n)
    east, west = lax.rem(lon + 1, lon_n), lax.rem(lon + lon_n - 1, lon_n)

    barrier = pltpu.get_barrier_semaphore()
    peers = [(a, b) for a in (lat, north, south) for b in (lon, east, west)][1:]
    for peer in peers:
        pl.semaphore_signal(barrier, inc=1, device_id=peer, device_id_type=MESH)

    count = [0]

    def fetch(src, dst):
        copy = pltpu.make_async_copy(src, dst, local_sem.at[count[0]])
        count[0] += 1
        copy.start()
        return copy

    def half(h):
        return pl.ds(h * LANES, LANES)

    inner = pl.ds(TOP, R)
    small = []
    for h in range(2):
        small.append(fetch(ocn.at[:, half(h)], oc.at[h]))
        small.append(fetch(srf.at[:, half(h)], ext.at[SURF, h, inner]))
        small.append(fetch(dmp.at[:, half(h)], ext.at[DAMP, h, inner]))
    vel_copies = []
    for c in range(2):
        for h in range(2):
            here = pl.ds(c * L * R, L * R)
            vel_copies.append((c, h, fetch(
                vel.at[here, half(h)], vb.at[h, pl.ds(8 + c * L * R, L * R)])))
    tra_copies = [fetch(tra.at[:, half(h)], tb.at[h, pl.ds(8, 2 * L * R)]) for h in range(2)]

    zero8 = jnp.zeros((8, LANES), jnp.float32)
    for h in range(2):
        for buf, size in ((vb, 2 * L * R), (tb, 2 * L * R), (pb, L * R)):
            buf[h, 0:8] = zero8
            buf[h, 8 + size:16 + size] = zero8

    for copy in small:
        copy.wait()
    for h in range(2):
        ext[MASK, h, TOP:TOP + R] = oc[h].astype(jnp.float32)

    mid = R // 2
    lane_m = lanes_of(mid)

    def pack_cols(field, acc_w, acc_e):
        off = HALO * field
        for part in range(2):
            at = off + 64 * part
            keep = (lane_m >= at) & (lane_m < at + HALO)
            rows_here = slice(TOP + mid * part, TOP + mid * (part + 1))
            acc_w = jnp.where(keep, shift(ext[field, 0, rows_here], at), acc_w)
            acc_e = jnp.where(keep, shift(ext[field, 1, rows_here], at + HALO), acc_e)
        return acc_w, acc_e

    def pack_rows(field):
        for h in range(2):
            msg_n[h, 8 * field:8 * field + 8] = ext[field, h, TOP + R - 8:TOP + R]
            msg_s[h, 8 * field:8 * field + 8] = ext[field, h, TOP:TOP + 8]

    far = ((SURF, 0), (MASK, 1), (VSUM, 2))

    def pack_far(field, place):
        for h in range(2):
            msg_n[h, 40 + place:41 + place] = ext[field, h, TOP + R - 9:TOP + R - 8]
            msg_s[h, 40 + place:41 + place] = ext[field, h, TOP + 8:TOP + 9]

    for h in range(2):
        msg_n[h, 40:48] = zero8
        msg_s[h, 40:48] = zero8
    accs = (jnp.zeros((mid, LANES), jnp.float32),) * 2
    for field in (SURF, MASK, DAMP):
        accs = pack_cols(field, *accs)
        pack_rows(field)
    pack_far(*far[0])
    pack_far(*far[1])
    msg_w[...], msg_e[...] = accs

    thick = [2.0 * (k + 1.0) / (L * (L + 1)) for k in range(L)]
    for c, h, copy in vel_copies:
        copy.wait()
        total = None
        for k in range(L):
            at = 8 + (c * L + k) * R
            term = thick[k] * vb[h, at:at + R]
            total = term if total is None else total + term
        ext[USUM + c, h, TOP:TOP + R] = total
    accs = (msg_w[...], msg_e[...])
    for field in (USUM, VSUM):
        accs = pack_cols(field, *accs)
        pack_rows(field)
    pack_far(*far[2])
    msg_w[...], msg_e[...] = accs

    def remote(i, src, dst, peer):
        return pltpu.make_async_remote_copy(
            src_ref=src, dst_ref=dst, send_sem=send_sem.at[i], recv_sem=recv_sem.at[i],
            device_id=peer, device_id_type=MESH)

    urgent = [
        remote(0, msg_e, got_w, (lat, east)),
        remote(1, msg_w, got_e, (lat, west)),
        remote(2, msg_e.at[pl.ds(mid - 8, 8)], corner.at[3], (north, east)),
        remote(3, msg_w.at[pl.ds(mid - 8, 8)], corner.at[2], (north, west)),
        remote(4, msg_e.at[pl.ds(0, 8)], corner.at[1], (south, east)),
        remote(5, msg_w.at[pl.ds(0, 8)], corner.at[0], (south, west)),
        remote(6, msg_n, got_s, (north, lon)),
        remote(7, msg_s, got_n, (south, lon)),
    ]
    late = [
        remote(8, col_e, gcol_w, (lat, east)),
        remote(9, col_w, gcol_e, (lat, west)),
        remote(10, row_n, grow_s, (north, lon)),
        remote(11, row_s, grow_n, (south, lon)),
    ]

    ahead = lon == 0

    @pl.when(jnp.logical_not(ahead))
    def _():
        pl.semaphore_wait(barrier, 8)
        for copy in urgent:
            copy.start()

    scale = 0.5 * time_step
    lane_r = lanes_of(R)
    first_r, last_r = lane_r == 0, lane_r == LANES - 1
    row_r = lax.broadcasted_iota(jnp.int32, (R, LANES), 0)
    m = [ext[MASK, h, TOP:TOP + R] for h in range(2)]
    m_east, m_west = east_of(m, last_r), west_of(m, first_r)
    j = (row_r + lat * R).astype(jnp.float32)
    planet = coriolis * (2.0 * (j + 0.5) / (R * lat_n) - 1.0)
    for h in range(2):
        fe, fw = m[h] * m_east[h], m[h] * m_west[h]
        if h == 1:
            fe = jnp.where(last_r, 0.0, fe)
        else:
            fw = jnp.where(first_r, 0.0, fw)
        fn = jnp.where(row_r == R - 1, 0.0, m[h] * pltpu.roll(m[h], R - 1, 0))
        fs = jnp.where(row_r == 0, 0.0, m[h] * pltpu.roll(m[h], 1, 0))
        fe, fw, fn, fs = scale * fe, scale * fw, scale * fn, scale * fs
        closed = ((fe + fw) + (fn + fs))
        for i, value in enumerate((fe, fw, fn, fs, m[h] - closed, time_step * planet * m[h],
                                   fe - fw, fn - fs, 1.0 - closed)):
            cf[i, h] = value

    for copy in tra_copies:
        copy.wait()
    for h in range(2):
        press = None
        for k in range(L):
            at = 8 + k * R
            warm = (buoyancy * thermal * thick[k]) * tb[h, at:at + R]
            salt = (buoyancy * haline * thick[k]) * tb[h, at + L * R:at + L * R + R]
            press = warm - salt if press is None else press + (warm - salt)
            pb[h, at:at + R] = press

    stacks = ((vb, 0), (vb, 1), (tb, 0), (tb, 1), (pb, 0))

    def pack_level(k, accs):
        acc_w, acc_e = accs
        for f, (buf, c) in enumerate(stacks):
            at = pl.multiple_of(8 + (c * L + k) * R, 8)
            lane = f * L + k
            both = jnp.where(last_r, buf[1, pl.ds(at, R)], buf[0, pl.ds(at, R)])
            both = shift(both, lane)
            acc_w = jnp.where(lane_r == lane, both, acc_w)
            acc_e = jnp.where(lane_r == ((lane - 1) & (LANES - 1)), both, acc_e)
        return acc_w, acc_e

    zero_r = jnp.zeros((R, LANES), jnp.float32)
    col_w[...], col_e[...] = lax.fori_loop(0, L, pack_level, (zero_r, zero_r), unroll=2)
    for h in range(2):
        for out, row in ((row_n, R - 1), (row_s, 0)):
            out[h, 5 * L // 8 * 8:] = zero8
            for buf, base, n in ((vb, 0, 2 * L), (tb, 2 * L, 2 * L), (pb, 4 * L, L)):
                for k in range(0, n, 8):
                    size = min(8, n - k)
                    out[h, base + k:base + k + size] = buf[h, pl.ds(8 + row + k * R, size, stride=R)]

    @pl.when(jnp.logical_not(ahead))
    def _():
        for copy in late:
            copy.start()

    lane_8 = lanes_of(8)
    first, last = lane_8 == 0, lane_8 == LANES - 1

    def level(k, carry):
        at_u = pl.multiple_of(k * R, R)
        at_v = pl.multiple_of((L + k) * R, R)

        def views(buf, at):
            return [buf.at[h, pl.ds(at, R + 16)] for h in range(2)]

        uv, vv = views(vb, at_u), views(vb, at_v)
        tv, sv = views(tb, at_u), views(tb, at_v)
        pv = views(pb, at_u)
        for r in range(0, R, 8):
            def get(view, by=0):
                return [view[h][8 + r + by:16 + r + by] for h in range(2)]

            fe, fw, fn, fs, mid_v, fc, fx, fy, mid_t = [
                [cf[i, h, r:r + 8] for h in range(2)] for i in range(9)]
            u, v, p = get(uv), get(vv), get(pv)
            te = [fe[h] - fe[h] * u[h] for h in range(2)]
            tw = [fw[h] + fw[h] * u[h] for h in range(2)]
            tn = [fn[h] - fn[h] * v[h] for h in range(2)]
            ts = [fs[h] + fs[h] * v[h] for h in range(2)]
            tc = [mid_t[h] + (fx[h] * u[h] + fy[h] * v[h]) for h in range(2)]
            for view, at in ((tv, at_u), (sv, at_v)):
                q, qn, qs = get(view), get(view, 1), get(view, -1)
                qe, qw = east_of(q, last), west_of(q, first)
                for h in range(2):
                    to[h, pl.ds(at + r, 8)] = (
                        (te[h] * qe[h] + tw[h] * qw[h]) + (tn[h] * qn[h] + ts[h] * qs[h])) + tc[h] * q[h]
            un, us = get(uv, 1), get(uv, -1)
            less_e = east_of([u[h] - p[h] for h in range(2)], last)
            more_w = west_of([u[h] + p[h] for h in range(2)], first)
            for h in range(2):
                vo[h, pl.ds(at_u + r, 8)] = (
                    ((fe[h] * less_e[h] + fw[h] * more_w[h]) + (fn[h] * un[h] + fs[h] * us[h]))
                    + ((mid_v[h] * u[h] + fx[h] * p[h]) + fc[h] * v[h]))
            vn, vs, pn, ps = get(vv, 1), get(vv, -1), get(pv, 1), get(pv, -1)
            ve, vw = east_of(v, last), west_of(v, first)
            for h in range(2):
                less_n, more_s = vn[h] - pn[h], vs[h] + ps[h]
                vo[h, pl.ds(at_v + r, 8)] = (
                    ((fe[h] * ve[h] + fw[h] * vw[h]) + (fn[h] * less_n + fs[h] * more_s))
                    + ((mid_v[h] * v[h] + fy[h] * p[h]) - fc[h] * u[h]))
        return carry

    lax.fori_loop(0, MEET, level, 0)

    @pl.when(ahead)
    def _():
        pl.semaphore_wait(barrier, 8)
        for copy in urgent + late:
            copy.start()

    lax.fori_loop(MEET, L, level, 0)

    late[2].wait_recv()
    late[3].wait_recv()
    keep_s = jnp.where(lat == 0, 0.0, 1.0)
    keep_n = jnp.where(lat == lat_n - 1, 0.0, 1.0)
    urgent[6].wait_recv()
    urgent[7].wait_recv()
    for h in range(2):
        mask_n = (scale * keep_n) * (ext[MASK, h, TOP + R - 1:TOP + R] * got_n[h, 8 * MASK:8 * MASK + 1])
        mask_s = (scale * keep_s) * (ext[MASK, h, TOP:TOP + 1] * got_s[h, 8 * MASK + 7:8 * MASK + 8])

        def parts(f):
            return slice(f * L, (f + 1) * L)

        gn = [mask_n * (grow_n[h, parts(f)] - row_n[h, parts(f)]) for f in range(5)]
        gs = [mask_s * (row_s[h, parts(f)] - grow_s[h, parts(f)]) for f in range(5)]
        vn, vs = row_n[h, parts(1)], row_s[h, parts(1)]
        fix_n = (gn[0], gn[1] - gn[4], gn[2] * (1.0 - vn), gn[3] * (1.0 - vn))
        fix_s = (-gs[0], -(gs[1] + gs[4]), -gs[2] * (1.0 + vs), -gs[3] * (1.0 + vs))
        for f in range(4):
            out, c = (vo, f) if f < 2 else (to, f - 2)
            for part, row in ((fix_n[f], R - 1), (fix_s[f], 0)):
                for k in range(0, L, 8):
                    size = min(8, L - k)
                    at = pl.ds((c * L + k) * R + row, size, stride=R)
                    out[h, at] = out[h, at] + part[k:k + size]

    for copy in urgent[:6]:
        copy.wait_recv()
    low, high = TOP - 8, TOP + R
    low_m, low_8 = lane_m < 64, lane_8 < 64
    for f in range(5):
        off = HALO * f
        ks, kn = (keep_s, keep_n) if f == MASK else (1.0, 1.0)
        for h in range(2):
            ext[f, h, low:low + 8] = got_s[h, 8 * f:8 * f + 8] * ks
            ext[f, h, high:high + 8] = got_n[h, 8 * f:8 * f + 8] * kn
        for part in range(2):
            at = off + 64 * part
            ext[f, 2, TOP + mid * part:TOP + mid * (part + 1)] = jnp.where(
                low_m, shift(got_e[...], -at), shift(got_w[...], LANES - HALO - at))
        ext[f, 2, high:high + 8] = kn * jnp.where(
            low_8, shift(corner[0], -off), shift(corner[1], LANES - HALO - off))
        ext[f, 2, low:low + 8] = ks * jnp.where(
            low_8, shift(corner[2], -off - 64), shift(corner[3], LANES - HALO - off - 64))
    for f, place in far:
        ks, kn = (keep_s, keep_n) if f == MASK else (1.0, 1.0)
        for h in range(2):
            ext[f, h, low - 1:low] = got_s[h, 40 + place:41 + place] * ks
            ext[f, h, high + 8:high + 9] = got_n[h, 40 + place:41 + place] * kn

    step = 16
    lane_s = lanes_of(step)
    first_s, last_s = lane_s == 0, lane_s == LANES - 1
    for r in range(0, R + 16, step):
        def near(f, by=0):
            return [ext[f, t, low + r + by:low + r + by + step] for t in range(3)]

        mm, mn, msth = near(MASK), near(MASK, 1), near(MASK, -1)
        me, mw = east_of(mm, last_s), west_of(mm, first_s)
        us, vs, vn, vso = near(USUM), near(VSUM), near(VSUM, 1), near(VSUM, -1)
        ue, uw = east_of(us, last_s), west_of(us, first_s)
        ss, ds = near(SURF), near(DAMP)
        for t in range(3):
            fe, fw, fn, fs = mm[t] * me[t], mm[t] * mw[t], mm[t] * mn[t], mm[t] * msth[t]
            column = 0.5 * ((fe * (ue[t] + us[t]) - fw * (us[t] + uw[t]))
                            + (fn * (vn[t] + vs[t]) - fs * (vs[t] + vso[t])))
            forcing = ds[t] * ss[t] - transport * column
            inv = 1.0 / (ds[t] + fe + fw + fn + fs)
            for i, value in enumerate((forcing, fe, fw, fn, fs)):
                co[i, t, r:r + step] = value * inv

    for n, (wa, wc) in enumerate(sweep_weights(SWEEPS)):
        def rd(t, at, n=n):
            return ext[SURF, t, at:at + step] if n % 2 == 0 else xb[t, at:at + step]

        for r in range(0, R + 16, step):
            at = low + r
            x = [rd(t, at) for t in range(3)]
            xe, xw = east_of(x, last_s), west_of(x, first_s)
            for t in range(3):
                g, ce, cw, cn, cs = [co[i, t, r:r + step] for i in range(5)]
                resid = (((g - x[t]) + ce * xe[t]) + (cw * xw[t] + cn * rd(t, at + 1))) + cs * rd(t, at - 1)
                move = wc * resid
                if n > 0:
                    move = move + wa * dd[t, r:r + step]
                dd[t, r:r + step] = move
                if n % 2 == 0:
                    xb[t, at:at + step] = x[t] + move
                else:
                    ext[SURF, t, at:at + step] = x[t] + move

    push = 0.5 * time_step * gravity
    for r in range(0, R, step):
        def near(f, by=0):
            return [ext[f, t, TOP + r + by:TOP + r + by + step] for t in range(3)]

        mm, mn, msth = near(MASK), near(MASK, 1), near(MASK, -1)
        me, mw = east_of(mm, last_s), west_of(mm, first_s)
        x, xn, xs = near(SURF), near(SURF, 1), near(SURF, -1)
        xe, xw = east_of(x, last_s), west_of(x, first_s)
        for h in range(2):
            k = push * mm[h]
            cuv[0, h, r:r + step] = k * (me[h] * (xe[h] - x[h]) + mw[h] * (x[h] - xw[h]))
            cuv[1, h, r:r + step] = k * (mn[h] * (xn[h] - x[h]) + msth[h] * (x[h] - xs[h]))
            so[h, r:r + step] = x[h]

    late[0].wait_recv()
    late[1].wait_recv()
    mask_e = ext[MASK, 1, TOP:TOP + R][:, LANES - 1:] * ext[MASK, 2, TOP:TOP + R][:, :1]
    mask_w = ext[MASK, 0, TOP:TOP + R][:, :1] * ext[MASK, 2, TOP:TOP + R][:, LANES - 1:]
    own_e, own_w = shift(col_e[...], 1), col_w[...]
    g_e = (scale * mask_e) * (gcol_e[...] - own_e)
    g_w = (scale * mask_w) * (own_w - shift(gcol_w[...], 1))

    def beside(own):
        return jnp.where(lane_r < 3 * L, shift(own, 2 * L), shift(own, 3 * L))

    def choose(u_part, v_part, t_part):
        return jnp.where(lane_r < L, u_part, jnp.where(lane_r < 2 * L, v_part, t_part))

    fix_e = choose(g_e - shift(g_e, -4 * L), g_e, g_e * (1.0 - beside(own_e)))
    fix_w = -choose(g_w + shift(g_w, -4 * L), g_w, g_w * (1.0 + beside(own_w)))
    fix[0] = shift(fix_e, -1)
    fix[1] = fix_w

    for copy in urgent + late:
        copy.wait_send()


def write_kernel(
    levels, rows, vo, to, cuv, so, fix, vel_next, tra_next, srf_next, vbuf, tbuf, sem,
):
    L, R = levels, rows
    copies = []

    def put(src, dst):
        copy = pltpu.make_async_copy(src, dst, sem.at[len(copies)])
        copy.start()
        copies.append(copy)

    def half(h):
        return pl.ds(h * LANES, LANES)

    for h in range(2):
        put(so.at[h], srf_next.at[:, half(h)])
    lane_r = lanes_of(R)
    first_r, last_r = lane_r == 0, lane_r == LANES - 1
    chunk = L // PIECES
    for f in (2, 3, 0, 1):
        c = f % 2
        src, buf, out = (vo, vbuf, vel_next) if f < 2 else (to, tbuf, tra_next)
        for k0 in range(0, L, chunk):
            for k in range(k0, k0 + chunk):
                at = (c * L + k) * R
                lane = f * L + k
                edge = shift(jnp.where(lane_r == lane, fix[1], fix[0]), -lane)
                for h in range(2):
                    value = src[h, at:at + R]
                    if f < 2:
                        value = value - cuv[c, h]
                    buf[h, at:at + R] = jnp.where(last_r if h else first_r, value + edge, value)
            here = pl.ds((c * L + k0) * R, chunk * R)
            for h in range(2):
                put(buf.at[h, here], out.at[here, half(h)])
    for copy in copies:
        copy.wait()


def shards(lat_n, lon_n, velocity, tracer, surface, damping, ocean):
    _, L, R, C = velocity.shape
    f32 = jnp.float32
    anywhere = pl.BlockSpec(memory_space=pl.ANY)
    inside = pl.BlockSpec(memory_space=pltpu.VMEM)

    def scratch(*shape):
        return pltpu.VMEM(shape, f32)

    flat = 2 * L * R
    ring = R + 2 * TOP
    mid = [
        pltpu.VMEM((2, flat, LANES), f32),
        pltpu.VMEM((2, flat, LANES), f32),
        pltpu.VMEM((2, 2, R, LANES), f32),
        pltpu.VMEM((2, R, LANES), f32),
        pltpu.VMEM((2, R, LANES), f32),
    ]
    packed = 5 * L // 8 * 8 + 8
    made = pl.pallas_call(
        functools.partial(step_kernel, L, R, lat_n, lon_n),
        out_shape=mid,
        in_specs=[anywhere] * 5,
        out_specs=[inside] * 5,
        scratch_shapes=[
            scratch(2, flat + 16, LANES), scratch(2, flat + 16, LANES), scratch(2, L * R + 16, LANES),
            pltpu.VMEM((2, R, LANES), jnp.int32),
            scratch(5, 3, ring, LANES), scratch(3, ring, LANES), scratch(3, R + 16, LANES),
            scratch(5, 3, R + 16, LANES), scratch(9, 2, R, LANES),
            scratch(R // 2, LANES), scratch(R // 2, LANES), scratch(R // 2, LANES), scratch(R // 2, LANES),
            scratch(4, 8, LANES),
            scratch(2, 48, LANES), scratch(2, 48, LANES), scratch(2, 48, LANES), scratch(2, 48, LANES),
            scratch(R, LANES), scratch(R, LANES), scratch(R, LANES), scratch(R, LANES),
            scratch(2, packed, LANES), scratch(2, packed, LANES),
            scratch(2, packed, LANES), scratch(2, packed, LANES),
            pltpu.SemaphoreType.DMA((12,)),
            pltpu.SemaphoreType.DMA((12,)),
            pltpu.SemaphoreType.DMA((12,)),
        ],
        compiler_params=pltpu.CompilerParams(
            collective_id=0, has_side_effects=True, vmem_limit_bytes=32 * 1024 * 1024),
        name="ocean_step",
    )(*[
        pltpu.with_memory_space_constraint(x, pltpu.HBM)
        for x in (velocity.reshape(flat, C), tracer.reshape(flat, C), surface, damping, ocean)
    ])
    vel_next, tra_next, srf_next = pl.pallas_call(
        functools.partial(write_kernel, L, R),
        out_shape=[
            jax.ShapeDtypeStruct((flat, C), f32),
            jax.ShapeDtypeStruct((flat, C), f32),
            jax.ShapeDtypeStruct((R, C), f32),
        ],
        in_specs=[inside] * 5,
        out_specs=[anywhere] * 3,
        scratch_shapes=[scratch(2, flat, LANES), scratch(2, flat, LANES),
                        pltpu.SemaphoreType.DMA((2 + 8 * PIECES,))],
        compiler_params=pltpu.CompilerParams(vmem_limit_bytes=32 * 1024 * 1024),
        name="ocean_write",
    )(*made)
    return vel_next.reshape(velocity.shape), tra_next.reshape(tracer.shape), srf_next


def solution(mesh):
    placed = (
        P(None, None, "lat", "lon"),
        P(None, None, "lat", "lon"),
        P("lat", "lon"),
        P("lat", "lon"),
        P("lat", "lon"),
    )
    return jax.shard_map(
        functools.partial(shards, mesh.shape["lat"], mesh.shape["lon"]),
        mesh=mesh,
        in_specs=placed,
        out_specs=(P(None, None, "lat", "lon"), P(None, None, "lat", "lon"), P("lat", "lon")),
        check_vma=False,
    )
```

```python
import functools

import jax
import jax.numpy as jnp
from jax import lax
from jax.experimental import pallas as pl
from jax.experimental.pallas import tpu as pltpu
from jax.sharding import PartitionSpec as P

SWEEPS = 8

time_step = 0.2
gravity = 4.0
coriolis = 1.0
viscosity = 0.5
diffusivity = 0.5
thermal = 0.2
haline = 0.15
buoyancy = 2.0
transport = 1.0
damping_floor = 0.01

LANES = 128
PIECES = 2
HALO = 9
TOP = 16
MESH = pl.DeviceIdType.MESH
SURF, MASK, DAMP, USUM, VSUM = range(5)


def sweep_weights(count):
    low = damping_floor / (damping_floor + 4.0)
    high = 2.0 - low
    theta = (high + low) / 2.0
    delta = (high - low) / 2.0
    sigma = theta / delta
    weights = [(0.0, 1.0 / theta)]
    rho_now = 1.0 / sigma
    for _ in range(count - 1):
        rho_new = 1.0 / (2.0 * sigma - rho_now)
        weights.append((rho_new * rho_now, 2.0 * rho_new / delta))
        rho_now = rho_new
    return weights


def lanes_of(rows):
    return lax.broadcasted_iota(jnp.int32, (rows, LANES), 1)


def shift(x, by):
    if isinstance(by, int):
        by %= LANES
        if by == 0:
            return x
    return pltpu.roll(x, by, 1)


def east_of(q, last):
    r = [shift(x, -1) for x in q]
    n = len(q)
    if n == 1:
        return r
    return [jnp.where(last, r[(i + 1) % n], r[i]) for i in range(n)]


def west_of(q, first):
    r = [shift(x, 1) for x in q]
    n = len(q)
    if n == 1:
        return r
    return [jnp.where(first, r[(i - 1) % n], r[i]) for i in range(n)]


def step_kernel(
    levels, rows, lat_n, lon_n,
    vel, tra, srf, dmp, ocn,
    vo, to, cuv, so, fix,
    vb, tb, pb, oc, ext, xb, dd, co, cf, strip, sxb, sdd, sco,
    msg_e, msg_w, got_e, got_w, corner,
    msg_n, msg_s, got_n, got_s,
    col_e, col_w, gcol_e, gcol_w,
    row_n, row_s, grow_n, grow_s,
    local_sem, send_sem, recv_sem,
):
    L, R = levels, rows
    lat, lon = lax.axis_index("lat"), lax.axis_index("lon")
    north, south = lax.rem(lat + 1, lat_n), lax.rem(lat + lat_n - 1, lat_n)
    east, west = lax.rem(lon + 1, lon_n), lax.rem(lon + lon_n - 1, lon_n)

    barrier = pltpu.get_barrier_semaphore()

    ahead, behind = lon == 0, lon == lon_n - 1

    def greet(*peers):
        for peer in peers:
            pl.semaphore_signal(barrier, inc=1, device_id=peer, device_id_type=MESH)

    greet((north, west), (south, west))

    @pl.when(jnp.logical_not(behind))
    def _():
        greet((north, east), (south, east), (lat, east))

    greet((lat, west), (north, lon), (south, lon))

    count = [0]

    def fetch(src, dst):
        copy = pltpu.make_async_copy(src, dst, local_sem.at[count[0]])
        count[0] += 1
        copy.start()
        return copy

    def half(h):
        return pl.ds(h * LANES, LANES)

    inner = pl.ds(TOP, R)
    small = []
    for h in range(2):
        small.append(fetch(ocn.at[:, half(h)], oc.at[h]))
        small.append(fetch(srf.at[:, half(h)], ext.at[SURF, h, inner]))
        small.append(fetch(dmp.at[:, half(h)], ext.at[DAMP, h, inner]))
    vel_copies = []
    for c in range(2):
        for h in range(2):
            here = pl.ds(c * L * R, L * R)
            vel_copies.append((c, h, fetch(
                vel.at[here, half(h)], vb.at[h, pl.ds(8 + c * L * R, L * R)])))
    tra_copies = [fetch(tra.at[:, half(h)], tb.at[h, pl.ds(8, 2 * L * R)]) for h in range(2)]

    zero8 = jnp.zeros((8, LANES), jnp.float32)
    for h in range(2):
        for buf, size in ((vb, 2 * L * R), (tb, 2 * L * R), (pb, L * R)):
            buf[h, 0:8] = zero8
            buf[h, 8 + size:16 + size] = zero8

    for copy in small:
        copy.wait()
    for h in range(2):
        ext[MASK, h, TOP:TOP + R] = oc[h].astype(jnp.float32)

    mid = R // 2
    lane_m = lanes_of(mid)

    def pack_cols(field, acc_w, acc_e):
        off = HALO * field
        for part in range(2):
            at = off + 64 * part
            keep = (lane_m >= at) & (lane_m < at + HALO)
            rows_here = slice(TOP + mid * part, TOP + mid * (part + 1))
            acc_w = jnp.where(keep, shift(ext[field, 0, rows_here], at), acc_w)
            acc_e = jnp.where(keep, shift(ext[field, 1, rows_here], at + HALO), acc_e)
        return acc_w, acc_e

    def pack_rows(field):
        for h in range(2):
            msg_n[h, 8 * field:8 * field + 8] = ext[field, h, TOP + R - 8:TOP + R]
            msg_s[h, 8 * field:8 * field + 8] = ext[field, h, TOP:TOP + 8]

    far = ((SURF, 0), (MASK, 1), (VSUM, 2))

    def pack_far(field, place):
        for h in range(2):
            msg_n[h, 40 + place:41 + place] = ext[field, h, TOP + R - 9:TOP + R - 8]
            msg_s[h, 40 + place:41 + place] = ext[field, h, TOP + 8:TOP + 9]

    for h in range(2):
        msg_n[h, 40:48] = zero8
        msg_s[h, 40:48] = zero8
    accs = (jnp.zeros((mid, LANES), jnp.float32),) * 2
    for field in (SURF, MASK, DAMP):
        accs = pack_cols(field, *accs)
        pack_rows(field)
    pack_far(*far[0])
    pack_far(*far[1])
    msg_w[...], msg_e[...] = accs

    thick = [2.0 * (k + 1.0) / (L * (L + 1)) for k in range(L)]
    for c, h, copy in vel_copies:
        copy.wait()
        total = None
        for k in range(L):
            at = 8 + (c * L + k) * R
            term = thick[k] * vb[h, at:at + R]
            total = term if total is None else total + term
        ext[USUM + c, h, TOP:TOP + R] = total
    accs = (msg_w[...], msg_e[...])
    for field in (USUM, VSUM):
        accs = pack_cols(field, *accs)
        pack_rows(field)
    pack_far(*far[2])
    msg_w[...], msg_e[...] = accs

    def remote(i, src, dst, peer):
        return pltpu.make_async_remote_copy(
            src_ref=src, dst_ref=dst, send_sem=send_sem.at[i], recv_sem=recv_sem.at[i],
            device_id=peer, device_id_type=MESH)

    urgent = [
        remote(0, msg_e, got_w, (lat, east)),
        remote(1, msg_w, got_e, (lat, west)),
        remote(2, msg_e.at[pl.ds(mid - 8, 8)], corner.at[3], (north, east)),
        remote(3, msg_w.at[pl.ds(mid - 8, 8)], corner.at[2], (north, west)),
        remote(4, msg_e.at[pl.ds(0, 8)], corner.at[1], (south, east)),
        remote(5, msg_w.at[pl.ds(0, 8)], corner.at[0], (south, west)),
        remote(6, msg_n, got_s, (north, lon)),
        remote(7, msg_s, got_n, (south, lon)),
    ]
    late = [
        remote(8, col_e, gcol_w, (lat, east)),
        remote(9, col_w, gcol_e, (lat, west)),
        remote(10, row_n, grow_s, (north, lon)),
        remote(11, row_s, grow_n, (south, lon)),
    ]

    westward = [urgent[3], urgent[5], urgent[1]]

    def start(*copies):
        for copy in copies:
            copy.start()

    @pl.when(ahead)
    def _():
        pl.semaphore_wait(barrier, 5)

    @pl.when(jnp.logical_not(ahead))
    def _():
        pl.semaphore_wait(barrier, 8)
        start(*westward)

    start(urgent[2], urgent[4], urgent[0], urgent[6], urgent[7])

    for copy in tra_copies:
        copy.wait()
    for h in range(2):
        press = None
        for k in range(L):
            at = 8 + k * R
            warm = (buoyancy * thermal * thick[k]) * tb[h, at:at + R]
            salt = (buoyancy * haline * thick[k]) * tb[h, at + L * R:at + L * R + R]
            press = warm - salt if press is None else press + (warm - salt)
            pb[h, at:at + R] = press

    stacks = ((vb, 0), (vb, 1), (tb, 0), (tb, 1), (pb, 0))
    lane_r = lanes_of(R)
    first_r, last_r = lane_r == 0, lane_r == LANES - 1
    acc_w = acc_e = jnp.zeros((R, LANES), jnp.float32)
    for f, (buf, c) in enumerate(stacks):
        for k in range(L):
            at = 8 + (c * L + k) * R
            lane = f * L + k
            both = shift(jnp.where(last_r, buf[1, at:at + R], buf[0, at:at + R]), lane)
            acc_w = jnp.where(lane_r == lane, both, acc_w)
            acc_e = jnp.where(lane_r == (lane - 1) % LANES, both, acc_e)
    col_w[...], col_e[...] = acc_w, acc_e

    late[0].start()

    @pl.when(jnp.logical_not(ahead))
    def _():
        late[1].start()

    for h in range(2):
        for out, row in ((row_n, R - 1), (row_s, 0)):
            out[h, 5 * L // 8 * 8:] = zero8
            for buf, base, n in ((vb, 0, 2 * L), (tb, 2 * L, 2 * L), (pb, 4 * L, L)):
                for k in range(0, n, 8):
                    size = min(8, n - k)
                    out[h, base + k:base + k + size] = buf[h, pl.ds(8 + row + k * R, size, stride=R)]

    start(late[2], late[3])

    scale = 0.5 * time_step
    row_r = lax.broadcasted_iota(jnp.int32, (R, LANES), 0)
    m = [ext[MASK, h, TOP:TOP + R] for h in range(2)]
    m_east, m_west = east_of(m, last_r), west_of(m, first_r)
    j = (row_r + lat * R).astype(jnp.float32)
    planet = coriolis * (2.0 * (j + 0.5) / (R * lat_n) - 1.0)
    for h in range(2):
        fe, fw = m[h] * m_east[h], m[h] * m_west[h]
        if h == 1:
            fe = jnp.where(last_r, 0.0, fe)
        else:
            fw = jnp.where(first_r, 0.0, fw)
        fn = jnp.where(row_r == R - 1, 0.0, m[h] * pltpu.roll(m[h], R - 1, 0))
        fs = jnp.where(row_r == 0, 0.0, m[h] * pltpu.roll(m[h], 1, 0))
        fe, fw, fn, fs = scale * fe, scale * fw, scale * fn, scale * fs
        closed = ((fe + fw) + (fn + fs))
        for i, value in enumerate((fe, fw, fn, fs, m[h] - closed, time_step * planet * m[h],
                                   fe - fw, fn - fs, 1.0 - closed)):
            cf[i, h] = value

    lane_8 = lanes_of(8)
    first, last = lane_8 == 0, lane_8 == LANES - 1

    def level(k, carry):
        at_u = pl.multiple_of(k * R, R)
        at_v = pl.multiple_of((L + k) * R, R)

        def views(buf, at):
            return [buf.at[h, pl.ds(at, R + 16)] for h in range(2)]

        uv, vv = views(vb, at_u), views(vb, at_v)
        tv, sv = views(tb, at_u), views(tb, at_v)
        pv = views(pb, at_u)
        for r in range(0, R, 8):
            def get(view, by=0):
                return [view[h][8 + r + by:16 + r + by] for h in range(2)]

            fe, fw, fn, fs, mid_v, fc, fx, fy, mid_t = [
                [cf[i, h, r:r + 8] for h in range(2)] for i in range(9)]
            u, v, p = get(uv), get(vv), get(pv)
            te = [fe[h] - fe[h] * u[h] for h in range(2)]
            tw = [fw[h] + fw[h] * u[h] for h in range(2)]
            tn = [fn[h] - fn[h] * v[h] for h in range(2)]
            ts = [fs[h] + fs[h] * v[h] for h in range(2)]
            tc = [mid_t[h] + (fx[h] * u[h] + fy[h] * v[h]) for h in range(2)]
            for view, at in ((tv, at_u), (sv, at_v)):
                q, qn, qs = get(view), get(view, 1), get(view, -1)
                qe, qw = east_of(q, last), west_of(q, first)
                for h in range(2):
                    to[h, pl.ds(at + r, 8)] = (
                        (te[h] * qe[h] + tw[h] * qw[h]) + (tn[h] * qn[h] + ts[h] * qs[h])) + tc[h] * q[h]
            un, us = get(uv, 1), get(uv, -1)
            less_e = east_of([u[h] - p[h] for h in range(2)], last)
            more_w = west_of([u[h] + p[h] for h in range(2)], first)
            for h in range(2):
                vo[h, pl.ds(at_u + r, 8)] = (
                    ((fe[h] * less_e[h] + fw[h] * more_w[h]) + (fn[h] * un[h] + fs[h] * us[h]))
                    + ((mid_v[h] * u[h] + fx[h] * p[h]) + fc[h] * v[h]))
            vn, vs, pn, ps = get(vv, 1), get(vv, -1), get(pv, 1), get(pv, -1)
            ve, vw = east_of(v, last), west_of(v, first)
            for h in range(2):
                less_n, more_s = vn[h] - pn[h], vs[h] + ps[h]
                vo[h, pl.ds(at_v + r, 8)] = (
                    ((fe[h] * ve[h] + fw[h] * vw[h]) + (fn[h] * less_n + fs[h] * more_s))
                    + ((mid_v[h] * v[h] + fy[h] * p[h]) - fc[h] * u[h]))
        return carry

    lax.fori_loop(0, L, level, 0)

    keep_s = jnp.where(lat == 0, 0.0, 1.0)
    keep_n = jnp.where(lat == lat_n - 1, 0.0, 1.0)
    low, high = TOP - 8, TOP + R

    def keeps(f):
        return (keep_s, keep_n) if f == MASK else (1.0, 1.0)

    for i in (6, 7, 1, 5, 3):
        urgent[i].wait_recv()
    for f in range(5):
        off = HALO * f
        ks, kn = keeps(f)
        for h in range(2):
            ext[f, h, low:low + 8] = got_s[h, 8 * f:8 * f + 8] * ks
            ext[f, h, high:high + 8] = got_n[h, 8 * f:8 * f + 8] * kn
        for part in range(2):
            ext[f, 2, TOP + mid * part:TOP + mid * (part + 1)] = shift(got_e[...], -off - 64 * part)
        ext[f, 2, high:high + 8] = kn * shift(corner[0], -off)
        ext[f, 2, low:low + 8] = ks * shift(corner[2], -off - 64)
    for f, place in far:
        ks, kn = keeps(f)
        for h in range(2):
            ext[f, h, low - 1:low] = got_s[h, 40 + place:41 + place] * ks
            ext[f, h, high + 8:high + 9] = got_n[h, 40 + place:41 + place] * kn

    for f in range(5):
        for r in range(0, R + 2 * TOP, 16):
            strip[f, 0, r:r + 16] = shift(ext[f, 0, r:r + 16], 64)

    step = 16
    lane_s = lanes_of(step)
    first_s, last_s = lane_s == 0, lane_s == LANES - 1

    def solve(fld, other, run, coe, n):
        for r in range(0, R + 16, step):
            def near(f, by=0):
                return [fld[f, t, low + r + by:low + r + by + step] for t in range(n)]

            mm, mn, ms = near(MASK), near(MASK, 1), near(MASK, -1)
            me, mw = east_of(mm, last_s), west_of(mm, first_s)
            us, vs, vn, vso = near(USUM), near(VSUM), near(VSUM, 1), near(VSUM, -1)
            ue, uw = east_of(us, last_s), west_of(us, first_s)
            ss, ds = near(SURF), near(DAMP)
            for t in range(n):
                fe, fw, fn, fs = mm[t] * me[t], mm[t] * mw[t], mm[t] * mn[t], mm[t] * ms[t]
                column = 0.5 * ((fe * (ue[t] + us[t]) - fw * (us[t] + uw[t]))
                                + (fn * (vn[t] + vs[t]) - fs * (vs[t] + vso[t])))
                forcing = ds[t] * ss[t] - transport * column
                inv = 1.0 / (ds[t] + fe + fw + fn + fs)
                for i, value in enumerate((forcing, fe, fw, fn, fs)):
                    coe[i, t, r:r + step] = value * inv
        for sweep, (wa, wc) in enumerate(sweep_weights(SWEEPS)):
            even = sweep % 2 == 0

            def rd(t, at):
                return fld[SURF, t, at:at + step] if even else other[t, at:at + step]

            for r in range(0, R + 16, step):
                at = low + r
                x = [rd(t, at) for t in range(n)]
                xe, xw = east_of(x, last_s), west_of(x, first_s)
                for t in range(n):
                    g, ce, cw, cn, cs = [coe[i, t, r:r + step] for i in range(5)]
                    resid = (((g - x[t]) + ce * xe[t])
                             + (cw * xw[t] + cn * rd(t, at + 1))) + cs * rd(t, at - 1)
                    move = wc * resid
                    if sweep > 0:
                        move = move + wa * run[t, r:r + step]
                    run[t, r:r + step] = move
                    if even:
                        other[t, at:at + step] = x[t] + move
                    else:
                        fld[SURF, t, at:at + step] = x[t] + move

    push = 0.5 * time_step * gravity

    def gradient(fld, r, n, wanted):
        def near(f, by=0):
            return [fld[f, t, TOP + r + by:TOP + r + by + step] for t in range(n)]

        mm, mn, ms = near(MASK), near(MASK, 1), near(MASK, -1)
        me, mw = east_of(mm, last_s), west_of(mm, first_s)
        x, xn, xs = near(SURF), near(SURF, 1), near(SURF, -1)
        xe, xw = east_of(x, last_s), west_of(x, first_s)
        for h in range(wanted):
            k = push * mm[h]
            yield (k * (me[h] * (xe[h] - x[h]) + mw[h] * (x[h] - xw[h])),
                   k * (mn[h] * (xn[h] - x[h]) + ms[h] * (x[h] - xs[h])), x[h])

    solve(ext, xb, dd, co, 3)
    for r in range(0, R, step):
        for h, (du, dv, x) in enumerate(gradient(ext, r, 3, 2)):
            cuv[0, h, r:r + step] = du
            cuv[1, h, r:r + step] = dv
            so[h, r:r + step] = x

    late[2].wait_recv()
    late[3].wait_recv()
    for h in range(2):
        mask_n = scale * (ext[MASK, h, TOP + R - 1:TOP + R] * ext[MASK, h, TOP + R:TOP + R + 1])
        mask_s = scale * (ext[MASK, h, TOP:TOP + 1] * ext[MASK, h, TOP - 1:TOP])

        def parts(f):
            return slice(f * L, (f + 1) * L)

        gn = [mask_n * (grow_n[h, parts(f)] - row_n[h, parts(f)]) for f in range(5)]
        gs = [mask_s * (row_s[h, parts(f)] - grow_s[h, parts(f)]) for f in range(5)]
        vn, vs = row_n[h, parts(1)], row_s[h, parts(1)]
        fix_n = (gn[0], gn[1] - gn[4], gn[2] * (1.0 - vn), gn[3] * (1.0 - vn))
        fix_s = (-gs[0], -(gs[1] + gs[4]), -gs[2] * (1.0 + vs), -gs[3] * (1.0 + vs))
        for f in range(4):
            out, c = (vo, f) if f < 2 else (to, f - 2)
            for part, row in ((fix_n[f], R - 1), (fix_s[f], 0)):
                for k in range(0, L, 8):
                    size = min(8, L - k)
                    at = pl.ds((c * L + k) * R + row, size, stride=R)
                    out[h, at] = out[h, at] + part[k:k + size]

    def beside(own):
        return jnp.where(lane_r < 3 * L, shift(own, 2 * L), shift(own, 3 * L))

    def choose(u_part, v_part, t_part):
        return jnp.where(lane_r < L, u_part, jnp.where(lane_r < 2 * L, v_part, t_part))

    for i in (0, 4, 2):
        urgent[i].wait_recv()

    @pl.when(ahead)
    def _():
        start(*westward, late[1])

    low_m, low_8 = lane_m < 64, lane_8 < 64
    for f in range(5):
        to_halo = 64 - HALO - HALO * f
        ks, kn = keeps(f)
        for part in range(2):
            here = slice(TOP + mid * part, TOP + mid * (part + 1))
            strip[f, 0, here] = jnp.where(low_m, shift(got_w[...], to_halo - 64 * part), strip[f, 0, here])
        here = slice(high, high + 8)
        strip[f, 0, here] = jnp.where(low_8, kn * shift(corner[1], to_halo), strip[f, 0, here])
        here = slice(low, low + 8)
        strip[f, 0, here] = jnp.where(low_8, ks * shift(corner[3], to_halo - 64), strip[f, 0, here])
    solve(strip, sxb, sdd, sco, 1)
    edge = lane_s < 32
    for r in range(0, R, step):
        du, dv, x = next(gradient(strip, r, 1, 1))
        here = slice(r, r + step)
        cuv[0, 0, here] = jnp.where(edge, shift(du, 64), cuv[0, 0, here])
        cuv[1, 0, here] = jnp.where(edge, shift(dv, 64), cuv[1, 0, here])
        so[0, here] = jnp.where(edge, shift(x, 64), so[0, here])

    late[0].wait_recv()
    mask_w = strip[MASK, 0, TOP:TOP + R][:, 64:65] * strip[MASK, 0, TOP:TOP + R][:, 63:64]
    own_w = col_w[...]
    g_w = (scale * mask_w) * (own_w - shift(gcol_w[...], 1))
    fix[1] = -choose(g_w + shift(g_w, -4 * L), g_w, g_w * (1.0 + beside(own_w)))

    late[1].wait_recv()
    mask_e = ext[MASK, 1, TOP:TOP + R][:, LANES - 1:] * ext[MASK, 2, TOP:TOP + R][:, :1]
    own_e = shift(col_e[...], 1)
    g_e = (scale * mask_e) * (gcol_e[...] - own_e)
    fix[0] = shift(choose(g_e - shift(g_e, -4 * L), g_e, g_e * (1.0 - beside(own_e))), -1)

    for copy in urgent + late:
        copy.wait_send()


def write_kernel(
    levels, rows, vo, to, cuv, so, fix, vel_next, tra_next, srf_next, vbuf, tbuf, sem,
):
    L, R = levels, rows
    copies = []

    def put(src, dst):
        copy = pltpu.make_async_copy(src, dst, sem.at[len(copies)])
        copy.start()
        copies.append(copy)

    def half(h):
        return pl.ds(h * LANES, LANES)

    for h in range(2):
        put(so.at[h], srf_next.at[:, half(h)])
    lane_r = lanes_of(R)
    first_r, last_r = lane_r == 0, lane_r == LANES - 1
    chunk = L // PIECES
    for f in (2, 3, 0, 1):
        c = f % 2
        src, buf, out = (vo, vbuf, vel_next) if f < 2 else (to, tbuf, tra_next)
        for k0 in range(0, L, chunk):
            for k in range(k0, k0 + chunk):
                at = (c * L + k) * R
                lane = f * L + k
                edge = shift(jnp.where(lane_r == lane, fix[1], fix[0]), -lane)
                for h in range(2):
                    value = src[h, at:at + R]
                    if f < 2:
                        value = value - cuv[c, h]
                    buf[at:at + R, h * LANES:(h + 1) * LANES] = jnp.where(
                        last_r if h else first_r, value + edge, value)
            here = pl.ds((c * L + k0) * R, chunk * R)
            put(buf.at[here], out.at[here])
    for copy in copies:
        copy.wait()


def shards(lat_n, lon_n, velocity, tracer, surface, damping, ocean):
    _, L, R, C = velocity.shape
    f32 = jnp.float32
    anywhere = pl.BlockSpec(memory_space=pl.ANY)
    inside = pl.BlockSpec(memory_space=pltpu.VMEM)

    def scratch(*shape):
        return pltpu.VMEM(shape, f32)

    flat = 2 * L * R
    ring = R + 2 * TOP
    mid = [
        pltpu.VMEM((2, flat, LANES), f32),
        pltpu.VMEM((2, flat, LANES), f32),
        pltpu.VMEM((2, 2, R, LANES), f32),
        pltpu.VMEM((2, R, LANES), f32),
        pltpu.VMEM((2, R, LANES), f32),
    ]
    packed = 5 * L // 8 * 8 + 8
    made = pl.pallas_call(
        functools.partial(step_kernel, L, R, lat_n, lon_n),
        out_shape=mid,
        in_specs=[anywhere] * 5,
        out_specs=[inside] * 5,
        scratch_shapes=[
            scratch(2, flat + 16, LANES), scratch(2, flat + 16, LANES), scratch(2, L * R + 16, LANES),
            pltpu.VMEM((2, R, LANES), jnp.int32),
            scratch(5, 3, ring, LANES), scratch(3, ring, LANES), scratch(3, R + 16, LANES),
            scratch(5, 3, R + 16, LANES), scratch(9, 2, R, LANES),
            scratch(5, 1, ring, LANES), scratch(1, ring, LANES), scratch(1, R + 16, LANES),
            scratch(5, 1, R + 16, LANES),
            scratch(R // 2, LANES), scratch(R // 2, LANES), scratch(R // 2, LANES), scratch(R // 2, LANES),
            scratch(4, 8, LANES),
            scratch(2, 48, LANES), scratch(2, 48, LANES), scratch(2, 48, LANES), scratch(2, 48, LANES),
            scratch(R, LANES), scratch(R, LANES), scratch(R, LANES), scratch(R, LANES),
            scratch(2, packed, LANES), scratch(2, packed, LANES),
            scratch(2, packed, LANES), scratch(2, packed, LANES),
            pltpu.SemaphoreType.DMA((12,)),
            pltpu.SemaphoreType.DMA((12,)),
            pltpu.SemaphoreType.DMA((12,)),
        ],
        compiler_params=pltpu.CompilerParams(
            collective_id=0, has_side_effects=True, vmem_limit_bytes=32 * 1024 * 1024),
        name="ocean_step",
    )(*[
        pltpu.with_memory_space_constraint(x, pltpu.HBM)
        for x in (velocity.reshape(flat, C), tracer.reshape(flat, C), surface, damping, ocean)
    ])
    vel_next, tra_next, srf_next = pl.pallas_call(
        functools.partial(write_kernel, L, R),
        out_shape=[
            jax.ShapeDtypeStruct((flat, C), f32),
            jax.ShapeDtypeStruct((flat, C), f32),
            jax.ShapeDtypeStruct((R, C), f32),
        ],
        in_specs=[inside] * 5,
        out_specs=[anywhere] * 3,
        scratch_shapes=[scratch(flat, C), scratch(flat, C), pltpu.SemaphoreType.DMA((2 + 4 * PIECES,))],
        compiler_params=pltpu.CompilerParams(vmem_limit_bytes=32 * 1024 * 1024),
        name="ocean_write",
    )(*made)
    return vel_next.reshape(velocity.shape), tra_next.reshape(tracer.shape), srf_next


def solution(mesh):
    placed = (
        P(None, None, "lat", "lon"),
        P(None, None, "lat", "lon"),
        P("lat", "lon"),
        P("lat", "lon"),
        P("lat", "lon"),
    )
    return jax.shard_map(
        functools.partial(shards, mesh.shape["lat"], mesh.shape["lon"]),
        mesh=mesh,
        in_specs=placed,
        out_specs=(P(None, None, "lat", "lon"), P(None, None, "lat", "lon"), P("lat", "lon")),
        check_vma=False,
    )
```

```python
import functools

import jax
import jax.numpy as jnp
from jax import lax
from jax.experimental import pallas as pl
from jax.experimental.pallas import tpu as pltpu
from jax.sharding import PartitionSpec as P

SWEEPS = 8

time_step = 0.2
gravity = 4.0
coriolis = 1.0
viscosity = 0.5
diffusivity = 0.5
thermal = 0.2
haline = 0.15
buoyancy = 2.0
transport = 1.0
damping_floor = 0.01

LANES = 128
PIECES = 2
MEET = 15
HALO = 9
TOP = 16
MESH = pl.DeviceIdType.MESH
SURF, MASK, DAMP, USUM, VSUM = range(5)


def sweep_weights(count):
    low = damping_floor / (damping_floor + 4.0)
    high = 2.0 - low
    theta = (high + low) / 2.0
    delta = (high - low) / 2.0
    sigma = theta / delta
    weights = [(0.0, 1.0 / theta)]
    rho_now = 1.0 / sigma
    for _ in range(count - 1):
        rho_new = 1.0 / (2.0 * sigma - rho_now)
        weights.append((rho_new * rho_now, 2.0 * rho_new / delta))
        rho_now = rho_new
    return weights


def lanes_of(rows):
    return lax.broadcasted_iota(jnp.int32, (rows, LANES), 1)


def shift(x, by):
    if isinstance(by, int):
        by %= LANES
        if by == 0:
            return x
    return pltpu.roll(x, by, 1)


def east_of(q, last):
    r = [shift(x, -1) for x in q]
    n = len(q)
    if n == 1:
        return r
    return [jnp.where(last, r[(i + 1) % n], r[i]) for i in range(n)]


def west_of(q, first):
    r = [shift(x, 1) for x in q]
    n = len(q)
    if n == 1:
        return r
    return [jnp.where(first, r[(i - 1) % n], r[i]) for i in range(n)]


def step_kernel(
    levels, rows, lat_n, lon_n,
    vel, tra, srf, dmp, ocn,
    vo, to, cuv, so, fix,
    vb, tb, pb, oc, ext, xb, dd, co, cf, strip, sxb, sdd, sco,
    msg_e, msg_w, got, corner,
    msg_n, msg_s, got_n, got_s,
    col_e, col_w, gcol_e, gcol_w,
    row_n, row_s, grow_n, grow_s,
    local_sem, send_sem, recv_sem, hello,
):
    L, R = levels, rows
    lat, lon = lax.axis_index("lat"), lax.axis_index("lon")
    north, south = lax.rem(lat + 1, lat_n), lax.rem(lat + lat_n - 1, lat_n)
    east, west = lax.rem(lon + 1, lon_n), lax.rem(lon + lon_n - 1, lon_n)

    barrier = pltpu.get_barrier_semaphore()

    first_col, last_col = lon == 0, lon == lon_n - 1
    few = first_col | last_col
    east_late = lon >= lon_n - 2
    side = jnp.where(east_late, 1, 0)

    def greet(*peers):
        for peer in peers:
            pl.semaphore_signal(barrier, inc=1, device_id=peer, device_id_type=MESH)

    greet((north, west), (south, west), (lat, west))

    @pl.when(jnp.logical_not(east_late))
    def _():
        greet((north, east), (south, east), (lat, east))

    greet((north, lon), (south, lon))

    count = [0]

    def fetch(src, dst):
        copy = pltpu.make_async_copy(src, dst, local_sem.at[count[0]])
        count[0] += 1
        copy.start()
        return copy

    def half(h):
        return pl.ds(h * LANES, LANES)

    inner = pl.ds(TOP, R)
    vel_copies, small = {}, {}
    for h in (1, 0):
        small[h] = [
            fetch(ocn.at[:, half(h)], oc.at[h]),
            fetch(srf.at[:, half(h)], ext.at[SURF, h, inner]),
            fetch(dmp.at[:, half(h)], ext.at[DAMP, h, inner]),
        ]
        for c in range(2):
            here = pl.ds(c * L * R, L * R)
            vel_copies[c, h] = fetch(vel.at[here, half(h)], vb.at[h, pl.ds(8 + c * L * R, L * R)])
    tra_copies = [fetch(tra.at[:, half(h)], tb.at[h, pl.ds(8, 2 * L * R)]) for h in range(2)]

    @pl.when(last_col)
    def _():
        pl.semaphore_wait(barrier, 5)
        for peer in ((north, east), (south, east), (lat, east)):
            pl.semaphore_signal(hello, inc=1, device_id=peer, device_id_type=MESH)

    zero8 = jnp.zeros((8, LANES), jnp.float32)
    for h in range(2):
        for buf, size in ((vb, 2 * L * R), (tb, 2 * L * R), (pb, L * R)):
            buf[h, 0:8] = zero8
            buf[h, 8 + size:16 + size] = zero8

    mid = R // 2
    lane_m = lanes_of(mid)
    thick = [2.0 * (k + 1.0) / (L * (L + 1)) for k in range(L)]

    def pack_cols(h, field, acc):
        off = HALO * field
        for part in range(2):
            at = off + 64 * part
            keep = (lane_m >= at) & (lane_m < at + HALO)
            rows_here = slice(TOP + mid * part, TOP + mid * (part + 1))
            acc = jnp.where(keep, shift(ext[field, h, rows_here], at + h * HALO), acc)
        return acc

    def urgent_half(h, out):
        for copy in small[h]:
            copy.wait()
        ext[MASK, h, TOP:TOP + R] = oc[h].astype(jnp.float32)
        acc = jnp.zeros((mid, LANES), jnp.float32)
        for field in (SURF, MASK, DAMP):
            acc = pack_cols(h, field, acc)
        for c in range(2):
            vel_copies[c, h].wait()
            total = None
            for k in range(L):
                at = 8 + (c * L + k) * R
                term = thick[k] * vb[h, at:at + R]
                total = term if total is None else total + term
            ext[USUM + c, h, TOP:TOP + R] = total
            acc = pack_cols(h, USUM + c, acc)
        out[...] = acc

    far = ((SURF, 0), (MASK, 1), (VSUM, 2))

    def remote(i, src, dst, peer):
        return pltpu.make_async_remote_copy(
            src_ref=src, dst_ref=dst, send_sem=send_sem.at[i], recv_sem=recv_sem.at[i],
            device_id=peer, device_id_type=MESH)

    urgent = [
        remote(0, msg_e, got.at[0], (lat, east)),
        remote(1, msg_w, got.at[1], (lat, west)),
        remote(2, msg_e.at[pl.ds(mid - 8, 8)], corner.at[3], (north, east)),
        remote(3, msg_w.at[pl.ds(mid - 8, 8)], corner.at[2], (north, west)),
        remote(4, msg_e.at[pl.ds(0, 8)], corner.at[1], (south, east)),
        remote(5, msg_w.at[pl.ds(0, 8)], corner.at[0], (south, west)),
        remote(6, msg_n, got_s, (north, lon)),
        remote(7, msg_s, got_n, (south, lon)),
    ]
    late = [
        remote(8, col_e, gcol_w, (lat, east)),
        remote(9, col_w, gcol_e, (lat, west)),
        remote(10, row_n, grow_s, (north, lon)),
        remote(11, row_s, grow_n, (south, lon)),
    ]

    westward = [urgent[3], urgent[5], urgent[1]]

    def start(*copies):
        for copy in copies:
            copy.start()

    urgent_half(1, msg_e)

    @pl.when(first_col)
    def _():
        pl.semaphore_wait(barrier, 5)

    @pl.when(jnp.logical_not(few))
    def _():
        pl.semaphore_wait(barrier, 8)

    start(urgent[2], urgent[4], urgent[0])
    urgent_half(0, msg_w)

    @pl.when(jnp.logical_not(few))
    def _():
        start(*westward)

    for h in range(2):
        for field in range(5):
            msg_n[h, 8 * field:8 * field + 8] = ext[field, h, TOP + R - 8:TOP + R]
            msg_s[h, 8 * field:8 * field + 8] = ext[field, h, TOP:TOP + 8]
        msg_n[h, 40:48] = zero8
        msg_s[h, 40:48] = zero8
        for field, place in far:
            msg_n[h, 40 + place:41 + place] = ext[field, h, TOP + R - 9:TOP + R - 8]
            msg_s[h, 40 + place:41 + place] = ext[field, h, TOP + 8:TOP + 9]
    start(urgent[6], urgent[7])

    for copy in tra_copies:
        copy.wait()
    for h in range(2):
        press = None
        for k in range(L):
            at = 8 + k * R
            warm = (buoyancy * thermal * thick[k]) * tb[h, at:at + R]
            salt = (buoyancy * haline * thick[k]) * tb[h, at + L * R:at + L * R + R]
            press = warm - salt if press is None else press + (warm - salt)
            pb[h, at:at + R] = press

    stacks = ((vb, 0), (vb, 1), (tb, 0), (tb, 1), (pb, 0))
    lane_r = lanes_of(R)
    first_r, last_r = lane_r == 0, lane_r == LANES - 1
    acc_w = acc_e = jnp.zeros((R, LANES), jnp.float32)
    for f, (buf, c) in enumerate(stacks):
        for k in range(L):
            at = 8 + (c * L + k) * R
            lane = f * L + k
            both = shift(jnp.where(last_r, buf[1, at:at + R], buf[0, at:at + R]), lane)
            acc_w = jnp.where(lane_r == lane, both, acc_w)
            acc_e = jnp.where(lane_r == (lane - 1) % LANES, both, acc_e)
    col_w[...], col_e[...] = acc_w, acc_e

    late[0].start()

    @pl.when(jnp.logical_not(few))
    def _():
        late[1].start()

    for h in range(2):
        for out, row in ((row_n, R - 1), (row_s, 0)):
            out[h, 5 * L // 8 * 8:] = zero8
            for buf, base, n in ((vb, 0, 2 * L), (tb, 2 * L, 2 * L), (pb, 4 * L, L)):
                for k in range(0, n, 8):
                    size = min(8, n - k)
                    out[h, base + k:base + k + size] = buf[h, pl.ds(8 + row + k * R, size, stride=R)]

    start(late[2], late[3])

    scale = 0.5 * time_step
    row_r = lax.broadcasted_iota(jnp.int32, (R, LANES), 0)
    m = [ext[MASK, h, TOP:TOP + R] for h in range(2)]
    m_east, m_west = east_of(m, last_r), west_of(m, first_r)
    j = (row_r + lat * R).astype(jnp.float32)
    planet = coriolis * (2.0 * (j + 0.5) / (R * lat_n) - 1.0)
    for h in range(2):
        fe, fw = m[h] * m_east[h], m[h] * m_west[h]
        if h == 1:
            fe = jnp.where(last_r, 0.0, fe)
        else:
            fw = jnp.where(first_r, 0.0, fw)
        fn = jnp.where(row_r == R - 1, 0.0, m[h] * pltpu.roll(m[h], R - 1, 0))
        fs = jnp.where(row_r == 0, 0.0, m[h] * pltpu.roll(m[h], 1, 0))
        fe, fw, fn, fs = scale * fe, scale * fw, scale * fn, scale * fs
        closed = ((fe + fw) + (fn + fs))
        for i, value in enumerate((fe, fw, fn, fs, m[h] - closed, time_step * planet * m[h],
                                   fe - fw, fn - fs, 1.0 - closed)):
            cf[i, h] = value

    lane_8 = lanes_of(8)
    first, last = lane_8 == 0, lane_8 == LANES - 1

    def level(k, carry):
        at_u = pl.multiple_of(k * R, R)
        at_v = pl.multiple_of((L + k) * R, R)

        def views(buf, at):
            return [buf.at[h, pl.ds(at, R + 16)] for h in range(2)]

        uv, vv = views(vb, at_u), views(vb, at_v)
        tv, sv = views(tb, at_u), views(tb, at_v)
        pv = views(pb, at_u)
        for r in range(0, R, 8):
            def get(view, by=0):
                return [view[h][8 + r + by:16 + r + by] for h in range(2)]

            fe, fw, fn, fs, mid_v, fc, fx, fy, mid_t = [
                [cf[i, h, r:r + 8] for h in range(2)] for i in range(9)]
            u, v, p = get(uv), get(vv), get(pv)
            te = [fe[h] - fe[h] * u[h] for h in range(2)]
            tw = [fw[h] + fw[h] * u[h] for h in range(2)]
            tn = [fn[h] - fn[h] * v[h] for h in range(2)]
            ts = [fs[h] + fs[h] * v[h] for h in range(2)]
            tc = [mid_t[h] + (fx[h] * u[h] + fy[h] * v[h]) for h in range(2)]
            for view, at in ((tv, at_u), (sv, at_v)):
                q, qn, qs = get(view), get(view, 1), get(view, -1)
                qe, qw = east_of(q, last), west_of(q, first)
                for h in range(2):
                    to[h, pl.ds(at + r, 8)] = (
                        (te[h] * qe[h] + tw[h] * qw[h]) + (tn[h] * qn[h] + ts[h] * qs[h])) + tc[h] * q[h]
            un, us = get(uv, 1), get(uv, -1)
            less_e = east_of([u[h] - p[h] for h in range(2)], last)
            more_w = west_of([u[h] + p[h] for h in range(2)], first)
            for h in range(2):
                vo[h, pl.ds(at_u + r, 8)] = (
                    ((fe[h] * less_e[h] + fw[h] * more_w[h]) + (fn[h] * un[h] + fs[h] * us[h]))
                    + ((mid_v[h] * u[h] + fx[h] * p[h]) + fc[h] * v[h]))
            vn, vs, pn, ps = get(vv, 1), get(vv, -1), get(pv, 1), get(pv, -1)
            ve, vw = east_of(v, last), west_of(v, first)
            for h in range(2):
                less_n, more_s = vn[h] - pn[h], vs[h] + ps[h]
                vo[h, pl.ds(at_v + r, 8)] = (
                    ((fe[h] * ve[h] + fw[h] * vw[h]) + (fn[h] * less_n + fs[h] * more_s))
                    + ((mid_v[h] * v[h] + fy[h] * p[h]) - fc[h] * u[h]))
        return carry

    def arrived(which):
        for i in which:
            urgent[i].wait_recv()

    from_west, from_east = (0, 4, 2), (1, 5, 3)
    lax.fori_loop(0, MEET, level, 0)

    @pl.when(last_col)
    def _():
        arrived(from_west)
        start(*westward, late[1])

    lax.fori_loop(MEET, L, level, 0)

    keep_s = jnp.where(lat == 0, 0.0, 1.0)
    keep_n = jnp.where(lat == lat_n - 1, 0.0, 1.0)
    low, high = TOP - 8, TOP + R

    def keeps(f):
        return (keep_s, keep_n) if f == MASK else (1.0, 1.0)

    arrived((6, 7))

    @pl.when(jnp.logical_not(east_late))
    def _():
        arrived(from_east)

    @pl.when(east_late & jnp.logical_not(last_col))
    def _():
        arrived(from_west)

    def turn(by):
        return lax.rem(by + 4 * LANES, LANES)

    to_end = side * (LANES - HALO)
    for f in range(5):
        off = HALO * f
        ks, kn = keeps(f)
        for h in range(2):
            ext[f, h, low:low + 8] = got_s[h, 8 * f:8 * f + 8] * ks
            ext[f, h, high:high + 8] = got_n[h, 8 * f:8 * f + 8] * kn
        for part in range(2):
            ext[f, 2, TOP + mid * part:TOP + mid * (part + 1)] = shift(
                got[1 - side], turn(to_end - off - 64 * part))
        ext[f, 2, high:high + 8] = kn * shift(corner[side], turn(to_end - off))
        ext[f, 2, low:low + 8] = ks * shift(corner[2 + side], turn(to_end - off - 64))
    for f, place in far:
        ks, kn = keeps(f)
        for h in range(2):
            ext[f, h, low - 1:low] = got_s[h, 40 + place:41 + place] * ks
            ext[f, h, high + 8:high + 9] = got_n[h, 40 + place:41 + place] * kn

    for f in range(5):
        for r in range(0, R + 2 * TOP, 16):
            strip[f, 0, r:r + 16] = shift(ext[f, side, r:r + 16], 64)

    step = 16
    lane_s = lanes_of(step)
    first_s, last_s = lane_s == 0, lane_s == LANES - 1

    def solve(fld, other, run, coe, n):
        for r in range(0, R + 16, step):
            def near(f, by=0):
                return [fld[f, t, low + r + by:low + r + by + step] for t in range(n)]

            mm, mn, ms = near(MASK), near(MASK, 1), near(MASK, -1)
            me, mw = east_of(mm, last_s), west_of(mm, first_s)
            us, vs, vn, vso = near(USUM), near(VSUM), near(VSUM, 1), near(VSUM, -1)
            ue, uw = east_of(us, last_s), west_of(us, first_s)
            ss, ds = near(SURF), near(DAMP)
            for t in range(n):
                fe, fw, fn, fs = mm[t] * me[t], mm[t] * mw[t], mm[t] * mn[t], mm[t] * ms[t]
                column = 0.5 * ((fe * (ue[t] + us[t]) - fw * (us[t] + uw[t]))
                                + (fn * (vn[t] + vs[t]) - fs * (vs[t] + vso[t])))
                forcing = ds[t] * ss[t] - transport * column
                inv = 1.0 / (ds[t] + fe + fw + fn + fs)
                for i, value in enumerate((forcing, fe, fw, fn, fs)):
                    coe[i, t, r:r + step] = value * inv
        for sweep, (wa, wc) in enumerate(sweep_weights(SWEEPS)):
            even = sweep % 2 == 0

            def rd(t, at):
                return fld[SURF, t, at:at + step] if even else other[t, at:at + step]

            for r in range(0, R + 16, step):
                at = low + r
                x = [rd(t, at) for t in range(n)]
                xe, xw = east_of(x, last_s), west_of(x, first_s)
                for t in range(n):
                    g, ce, cw, cn, cs = [coe[i, t, r:r + step] for i in range(5)]
                    resid = (((g - x[t]) + ce * xe[t])
                             + (cw * xw[t] + cn * rd(t, at + 1))) + cs * rd(t, at - 1)
                    move = wc * resid
                    if sweep > 0:
                        move = move + wa * run[t, r:r + step]
                    run[t, r:r + step] = move
                    if even:
                        other[t, at:at + step] = x[t] + move
                    else:
                        fld[SURF, t, at:at + step] = x[t] + move

    push = 0.5 * time_step * gravity

    def gradient(fld, r, n, wanted):
        def near(f, by=0):
            return [fld[f, t, TOP + r + by:TOP + r + by + step] for t in range(n)]

        mm, mn, ms = near(MASK), near(MASK, 1), near(MASK, -1)
        me, mw = east_of(mm, last_s), west_of(mm, first_s)
        x, xn, xs = near(SURF), near(SURF, 1), near(SURF, -1)
        xe, xw = east_of(x, last_s), west_of(x, first_s)
        for h in range(wanted):
            k = push * mm[h]
            yield (k * (me[h] * (xe[h] - x[h]) + mw[h] * (x[h] - xw[h])),
                   k * (mn[h] * (xn[h] - x[h]) + ms[h] * (x[h] - xs[h])), x[h])

    solve(ext, xb, dd, co, 3)
    for r in range(0, R, step):
        for h, (du, dv, x) in enumerate(gradient(ext, r, 3, 2)):
            cuv[0, h, r:r + step] = du
            cuv[1, h, r:r + step] = dv
            so[h, r:r + step] = x

    late[2].wait_recv()
    late[3].wait_recv()
    for h in range(2):
        mask_n = scale * (ext[MASK, h, TOP + R - 1:TOP + R] * ext[MASK, h, TOP + R:TOP + R + 1])
        mask_s = scale * (ext[MASK, h, TOP:TOP + 1] * ext[MASK, h, TOP - 1:TOP])

        def parts(f):
            return slice(f * L, (f + 1) * L)

        gn = [mask_n * (grow_n[h, parts(f)] - row_n[h, parts(f)]) for f in range(5)]
        gs = [mask_s * (row_s[h, parts(f)] - grow_s[h, parts(f)]) for f in range(5)]
        vn, vs = row_n[h, parts(1)], row_s[h, parts(1)]
        fix_n = (gn[0], gn[1] - gn[4], gn[2] * (1.0 - vn), gn[3] * (1.0 - vn))
        fix_s = (-gs[0], -(gs[1] + gs[4]), -gs[2] * (1.0 + vs), -gs[3] * (1.0 + vs))
        for f in range(4):
            out, c = (vo, f) if f < 2 else (to, f - 2)
            for part, row in ((fix_n[f], R - 1), (fix_s[f], 0)):
                for k in range(0, L, 8):
                    size = min(8, L - k)
                    at = pl.ds((c * L + k) * R + row, size, stride=R)
                    out[h, at] = out[h, at] + part[k:k + size]

    def beside(own):
        return jnp.where(lane_r < 3 * L, shift(own, 2 * L), shift(own, 3 * L))

    def choose(u_part, v_part, t_part):
        return jnp.where(lane_r < L, u_part, jnp.where(lane_r < 2 * L, v_part, t_part))

    def beyond(from_where, lane):
        pair = [got[from_where][:, at:at + 1] for at in (lane, lane + 64)]
        return jnp.concatenate(pair, axis=0)

    def fix_east():
        late[1].wait_recv()
        open_e = ext[MASK, 1, TOP:TOP + R][:, LANES - 1:] * beyond(1, HALO * MASK)
        own_e = shift(col_e[...], 1)
        g_e = (scale * open_e) * (gcol_e[...] - own_e)
        fix[0] = shift(choose(g_e - shift(g_e, -4 * L), g_e, g_e * (1.0 - beside(own_e))), -1)

    def fix_west():
        late[0].wait_recv()
        open_w = ext[MASK, 0, TOP:TOP + R][:, :1] * beyond(0, HALO * MASK + HALO - 1)
        own_w = col_w[...]
        g_w = (scale * open_w) * (own_w - shift(gcol_w[...], 1))
        fix[1] = -choose(g_w + shift(g_w, -4 * L), g_w, g_w * (1.0 + beside(own_w)))

    pl.when(jnp.logical_not(east_late))(fix_east)
    pl.when(east_late)(fix_west)

    @pl.when(first_col)
    def _():
        pl.semaphore_wait(hello, 3)
        start(*westward, late[1])

    @pl.when(jnp.logical_not(east_late))
    def _():
        arrived(from_west)

    @pl.when(east_late)
    def _():
        arrived(from_east)

    halo_m = lax.shift_right_logical(lane_m, 6) == side
    halo_8 = lax.shift_right_logical(lane_8, 6) == side
    for f in range(5):
        to_halo = 64 - HALO + HALO * side - HALO * f
        ks, kn = keeps(f)
        for part in range(2):
            here = slice(TOP + mid * part, TOP + mid * (part + 1))
            strip[f, 0, here] = jnp.where(
                halo_m, shift(got[side], turn(to_halo - 64 * part)), strip[f, 0, here])
        here = slice(high, high + 8)
        strip[f, 0, here] = jnp.where(
            halo_8, kn * shift(corner[1 - side], turn(to_halo)), strip[f, 0, here])
        here = slice(low, low + 8)
        strip[f, 0, here] = jnp.where(
            halo_8, ks * shift(corner[3 - side], turn(to_halo - 64)), strip[f, 0, here])
    solve(strip, sxb, sdd, sco, 1)
    edge = lax.shift_right_logical(lane_s, 5) == 3 * side
    for r in range(0, R, step):
        du, dv, x = next(gradient(strip, r, 1, 1))
        here = slice(r, r + step)
        cuv[0, side, here] = jnp.where(edge, shift(du, 64), cuv[0, side, here])
        cuv[1, side, here] = jnp.where(edge, shift(dv, 64), cuv[1, side, here])
        so[side, here] = jnp.where(edge, shift(x, 64), so[side, here])

    pl.when(jnp.logical_not(east_late))(fix_west)
    pl.when(east_late)(fix_east)

    for copy in urgent + late:
        copy.wait_send()


def write_kernel(
    levels, rows, vo, to, cuv, so, fix, vel_next, tra_next, srf_next, vbuf, tbuf, sem,
):
    L, R = levels, rows
    copies = []

    def put(src, dst):
        copy = pltpu.make_async_copy(src, dst, sem.at[len(copies)])
        copy.start()
        copies.append(copy)

    def half(h):
        return pl.ds(h * LANES, LANES)

    for h in range(2):
        put(so.at[h], srf_next.at[:, half(h)])
    lane_r = lanes_of(R)
    first_r, last_r = lane_r == 0, lane_r == LANES - 1
    chunk = L // PIECES
    for f in (2, 3, 0, 1):
        c = f % 2
        src, buf, out = (vo, vbuf, vel_next) if f < 2 else (to, tbuf, tra_next)
        for k0 in range(0, L, chunk):
            for k in range(k0, k0 + chunk):
                at = (c * L + k) * R
                lane = f * L + k
                edge = shift(jnp.where(lane_r == lane, fix[1], fix[0]), -lane)
                for h in range(2):
                    value = src[h, at:at + R]
                    if f < 2:
                        value = value - cuv[c, h]
                    buf[at:at + R, h * LANES:(h + 1) * LANES] = jnp.where(
                        last_r if h else first_r, value + edge, value)
            here = pl.ds((c * L + k0) * R, chunk * R)
            put(buf.at[here], out.at[here])
    for copy in copies:
        copy.wait()


def shards(lat_n, lon_n, velocity, tracer, surface, damping, ocean):
    _, L, R, C = velocity.shape
    f32 = jnp.float32
    anywhere = pl.BlockSpec(memory_space=pl.ANY)
    inside = pl.BlockSpec(memory_space=pltpu.VMEM)

    def scratch(*shape):
        return pltpu.VMEM(shape, f32)

    flat = 2 * L * R
    ring = R + 2 * TOP
    mid = [
        pltpu.VMEM((2, flat, LANES), f32),
        pltpu.VMEM((2, flat, LANES), f32),
        pltpu.VMEM((2, 2, R, LANES), f32),
        pltpu.VMEM((2, R, LANES), f32),
        pltpu.VMEM((2, R, LANES), f32),
    ]
    packed = 5 * L // 8 * 8 + 8
    made = pl.pallas_call(
        functools.partial(step_kernel, L, R, lat_n, lon_n),
        out_shape=mid,
        in_specs=[anywhere] * 5,
        out_specs=[inside] * 5,
        scratch_shapes=[
            scratch(2, flat + 16, LANES), scratch(2, flat + 16, LANES), scratch(2, L * R + 16, LANES),
            pltpu.VMEM((2, R, LANES), jnp.int32),
            scratch(5, 3, ring, LANES), scratch(3, ring, LANES), scratch(3, R + 16, LANES),
            scratch(5, 3, R + 16, LANES), scratch(9, 2, R, LANES),
            scratch(5, 1, ring, LANES), scratch(1, ring, LANES), scratch(1, R + 16, LANES),
            scratch(5, 1, R + 16, LANES),
            scratch(R // 2, LANES), scratch(R // 2, LANES), scratch(2, R // 2, LANES),
            scratch(4, 8, LANES),
            scratch(2, 48, LANES), scratch(2, 48, LANES), scratch(2, 48, LANES), scratch(2, 48, LANES),
            scratch(R, LANES), scratch(R, LANES), scratch(R, LANES), scratch(R, LANES),
            scratch(2, packed, LANES), scratch(2, packed, LANES),
            scratch(2, packed, LANES), scratch(2, packed, LANES),
            pltpu.SemaphoreType.DMA((12,)),
            pltpu.SemaphoreType.DMA((12,)),
            pltpu.SemaphoreType.DMA((12,)),
            pltpu.SemaphoreType.REGULAR,
        ],
        compiler_params=pltpu.CompilerParams(
            collective_id=0, has_side_effects=True, vmem_limit_bytes=32 * 1024 * 1024),
        name="ocean_step",
    )(*[
        pltpu.with_memory_space_constraint(x, pltpu.HBM)
        for x in (velocity.reshape(flat, C), tracer.reshape(flat, C), surface, damping, ocean)
    ])
    vel_next, tra_next, srf_next = pl.pallas_call(
        functools.partial(write_kernel, L, R),
        out_shape=[
            jax.ShapeDtypeStruct((flat, C), f32),
            jax.ShapeDtypeStruct((flat, C), f32),
            jax.ShapeDtypeStruct((R, C), f32),
        ],
        in_specs=[inside] * 5,
        out_specs=[anywhere] * 3,
        scratch_shapes=[scratch(flat, C), scratch(flat, C), pltpu.SemaphoreType.DMA((2 + 4 * PIECES,))],
        compiler_params=pltpu.CompilerParams(vmem_limit_bytes=32 * 1024 * 1024),
        name="ocean_write",
    )(*made)
    return vel_next.reshape(velocity.shape), tra_next.reshape(tracer.shape), srf_next


def solution(mesh):
    placed = (
        P(None, None, "lat", "lon"),
        P(None, None, "lat", "lon"),
        P("lat", "lon"),
        P("lat", "lon"),
        P("lat", "lon"),
    )
    return jax.shard_map(
        functools.partial(shards, mesh.shape["lat"], mesh.shape["lon"]),
        mesh=mesh,
        in_specs=placed,
        out_specs=(P(None, None, "lat", "lon"), P(None, None, "lat", "lon"), P("lat", "lon")),
        check_vma=False,
    )
```

```python
import functools

import jax
import jax.numpy as jnp
from jax import lax
from jax.experimental import pallas as pl
from jax.experimental.pallas import tpu as pltpu
from jax.sharding import PartitionSpec as P

SWEEPS = 8

time_step = 0.2
gravity = 4.0
coriolis = 1.0
viscosity = 0.5
diffusivity = 0.5
thermal = 0.2
haline = 0.15
buoyancy = 2.0
transport = 1.0
damping_floor = 0.01

LANES = 128
PIECES = 2
MEET = 15
HALO = 9
TOP = 16
MESH = pl.DeviceIdType.MESH
SURF, MASK, DAMP, USUM, VSUM = range(5)


def sweep_weights(count):
    low = damping_floor / (damping_floor + 4.0)
    high = 2.0 - low
    theta = (high + low) / 2.0
    delta = (high - low) / 2.0
    sigma = theta / delta
    weights = [(0.0, 1.0 / theta)]
    rho_now = 1.0 / sigma
    for _ in range(count - 1):
        rho_new = 1.0 / (2.0 * sigma - rho_now)
        weights.append((rho_new * rho_now, 2.0 * rho_new / delta))
        rho_now = rho_new
    return weights


def lanes_of(rows):
    return lax.broadcasted_iota(jnp.int32, (rows, LANES), 1)


def shift(x, by):
    if isinstance(by, int):
        by %= LANES
        if by == 0:
            return x
    return pltpu.roll(x, by, 1)


def east_of(q, last):
    r = [shift(x, -1) for x in q]
    n = len(q)
    if n == 1:
        return r
    return [jnp.where(last, r[(i + 1) % n], r[i]) for i in range(n)]


def west_of(q, first):
    r = [shift(x, 1) for x in q]
    n = len(q)
    if n == 1:
        return r
    return [jnp.where(first, r[(i - 1) % n], r[i]) for i in range(n)]


def step_kernel(
    levels, rows, lat_n, lon_n,
    vel, tra, srf, dmp, ocn, vel_levels,
    vo, to, cuv, so, fix,
    vb, tb, pb, oc, ext, xb, dd, co, cf, strip, sxb, sdd, sco,
    msg_e, msg_w, got, corner, ends, msg_c,
    msg_n, msg_s, got_n, got_s,
    col_e, col_w, gcol_e, gcol_w,
    row_n, row_s, grow_n, grow_s,
    local_sem, send_sem, recv_sem, hello,
):
    L, R = levels, rows
    lat, lon = lax.axis_index("lat"), lax.axis_index("lon")
    north, south = lax.rem(lat + 1, lat_n), lax.rem(lat + lat_n - 1, lat_n)
    east, west = lax.rem(lon + 1, lon_n), lax.rem(lon + lon_n - 1, lon_n)

    barrier = pltpu.get_barrier_semaphore()

    first_col, last_col = lon == 0, lon == lon_n - 1
    few = first_col | last_col
    east_late = lon >= lon_n - 2
    side = jnp.where(east_late, 1, 0)

    def greet(*peers):
        for peer in peers:
            pl.semaphore_signal(barrier, inc=1, device_id=peer, device_id_type=MESH)

    greet((north, west), (south, west), (lat, west))

    @pl.when(jnp.logical_not(east_late))
    def _():
        greet((north, east), (south, east), (lat, east))

    greet((north, lon), (south, lon))

    count = [0]

    def fetch(src, dst):
        copy = pltpu.make_async_copy(src, dst, local_sem.at[count[0]])
        count[0] += 1
        copy.start()
        return copy

    def half(h):
        return pl.ds(h * LANES, LANES)

    inner = pl.ds(TOP, R)
    vel_copies, small = {}, {}
    for h in (1, 0):
        small[h] = [
            fetch(ocn.at[:, half(h)], oc.at[h]),
            fetch(srf.at[:, half(h)], ext.at[SURF, h, inner]),
            fetch(dmp.at[:, half(h)], ext.at[DAMP, h, inner]),
        ]
        if h == 1:
            end_copies = [
                fetch(vel_levels.at[:, pl.ds(e * (R - 8), 8), half(1)], ends.at[e]) for e in range(2)]
        for c in range(2):
            here = pl.ds(c * L * R, L * R)
            vel_copies[c, h] = fetch(vel.at[here, half(h)], vb.at[h, pl.ds(8 + c * L * R, L * R)])
    tra_copies = [fetch(tra.at[:, half(h)], tb.at[h, pl.ds(8, 2 * L * R)]) for h in range(2)]

    @pl.when(last_col)
    def _():
        pl.semaphore_wait(barrier, 5)
        for peer in ((north, east), (south, east), (lat, east)):
            pl.semaphore_signal(hello, inc=1, device_id=peer, device_id_type=MESH)

    zero8 = jnp.zeros((8, LANES), jnp.float32)
    for h in range(2):
        for buf, size in ((vb, 2 * L * R), (tb, 2 * L * R), (pb, L * R)):
            buf[h, 0:8] = zero8
            buf[h, 8 + size:16 + size] = zero8

    mid = R // 2
    lane_m = lanes_of(mid)
    thick = [2.0 * (k + 1.0) / (L * (L + 1)) for k in range(L)]

    def pack_cols(h, field, acc):
        off = HALO * field
        for part in range(2):
            at = off + 64 * part
            keep = (lane_m >= at) & (lane_m < at + HALO)
            rows_here = slice(TOP + mid * part, TOP + mid * (part + 1))
            acc = jnp.where(keep, shift(ext[field, h, rows_here], at + h * HALO), acc)
        return acc

    def take_small(h):
        for copy in small[h]:
            copy.wait()
        ext[MASK, h, TOP:TOP + R] = oc[h].astype(jnp.float32)

    def urgent_half(h, out):
        if h == 0:
            take_small(0)
        acc = jnp.zeros((mid, LANES), jnp.float32)
        for field in (SURF, MASK, DAMP):
            acc = pack_cols(h, field, acc)
        for c in range(2):
            vel_copies[c, h].wait()
            total = None
            for k in range(L):
                at = 8 + (c * L + k) * R
                term = thick[k] * vb[h, at:at + R]
                total = term if total is None else total + term
            ext[USUM + c, h, TOP:TOP + R] = total
            acc = pack_cols(h, USUM + c, acc)
        out[...] = acc

    far = ((SURF, 0), (MASK, 1), (VSUM, 2))

    def remote(i, src, dst, peer):
        return pltpu.make_async_remote_copy(
            src_ref=src, dst_ref=dst, send_sem=send_sem.at[i], recv_sem=recv_sem.at[i],
            device_id=peer, device_id_type=MESH)

    urgent = [
        remote(0, msg_e, got.at[0], (lat, east)),
        remote(1, msg_w, got.at[1], (lat, west)),
        remote(2, msg_c.at[1], corner.at[3], (north, east)),
        remote(3, msg_w.at[pl.ds(mid - 8, 8)], corner.at[2], (north, west)),
        remote(4, msg_c.at[0], corner.at[1], (south, east)),
        remote(5, msg_w.at[pl.ds(0, 8)], corner.at[0], (south, west)),
        remote(6, msg_n, got_s, (north, lon)),
        remote(7, msg_s, got_n, (south, lon)),
    ]
    late = [
        remote(8, col_e, gcol_w, (lat, east)),
        remote(9, col_w, gcol_e, (lat, west)),
        remote(10, row_n, grow_s, (north, lon)),
        remote(11, row_s, grow_n, (south, lon)),
    ]

    westward = [urgent[3], urgent[5], urgent[1]]

    def start(*copies):
        for copy in copies:
            copy.start()

    take_small(1)
    lane_8 = lanes_of(8)
    for e in range(2):
        end_copies[e].wait()
        here = slice(TOP + e * (R - 8), TOP + e * (R - 8) + 8)
        fields = [ext[f, 1, here] for f in (SURF, MASK, DAMP)]
        for c in range(2):
            total = None
            for k in range(L):
                term = thick[k] * ends[e, c * L + k]
                total = term if total is None else total + term
            fields.append(total)
        acc = jnp.zeros((8, LANES), jnp.float32)
        for f, value in enumerate(fields):
            at = HALO * f + 64 * e
            acc = jnp.where((lane_8 >= at) & (lane_8 < at + HALO), shift(value, at + HALO), acc)
        msg_c[e] = acc

    @pl.when(last_col)
    def _():
        start(urgent[2], urgent[4])

    urgent_half(1, msg_e)

    @pl.when(first_col)
    def _():
        pl.semaphore_wait(barrier, 5)

    @pl.when(jnp.logical_not(few))
    def _():
        pl.semaphore_wait(barrier, 8)

    @pl.when(jnp.logical_not(last_col))
    def _():
        start(urgent[2], urgent[4])

    start(urgent[0])
    urgent_half(0, msg_w)

    @pl.when(jnp.logical_not(few))
    def _():
        start(*westward)

    for h in range(2):
        for field in range(5):
            msg_n[h, 8 * field:8 * field + 8] = ext[field, h, TOP + R - 8:TOP + R]
            msg_s[h, 8 * field:8 * field + 8] = ext[field, h, TOP:TOP + 8]
        msg_n[h, 40:48] = zero8
        msg_s[h, 40:48] = zero8
        for field, place in far:
            msg_n[h, 40 + place:41 + place] = ext[field, h, TOP + R - 9:TOP + R - 8]
            msg_s[h, 40 + place:41 + place] = ext[field, h, TOP + 8:TOP + 9]
    start(urgent[6], urgent[7])

    for copy in tra_copies:
        copy.wait()
    for h in range(2):
        press = None
        for k in range(L):
            at = 8 + k * R
            warm = (buoyancy * thermal * thick[k]) * tb[h, at:at + R]
            salt = (buoyancy * haline * thick[k]) * tb[h, at + L * R:at + L * R + R]
            press = warm - salt if press is None else press + (warm - salt)
            pb[h, at:at + R] = press

    stacks = ((vb, 0), (vb, 1), (tb, 0), (tb, 1), (pb, 0))
    lane_r = lanes_of(R)
    first_r, last_r = lane_r == 0, lane_r == LANES - 1
    acc_w = acc_e = jnp.zeros((R, LANES), jnp.float32)
    for f, (buf, c) in enumerate(stacks):
        for k in range(L):
            at = 8 + (c * L + k) * R
            lane = f * L + k
            both = shift(jnp.where(last_r, buf[1, at:at + R], buf[0, at:at + R]), lane)
            acc_w = jnp.where(lane_r == lane, both, acc_w)
            acc_e = jnp.where(lane_r == (lane - 1) % LANES, both, acc_e)
    col_w[...], col_e[...] = acc_w, acc_e

    late[0].start()

    @pl.when(jnp.logical_not(few))
    def _():
        late[1].start()

    for h in range(2):
        for out, row in ((row_n, R - 1), (row_s, 0)):
            out[h, 5 * L // 8 * 8:] = zero8
            for buf, base, n in ((vb, 0, 2 * L), (tb, 2 * L, 2 * L), (pb, 4 * L, L)):
                for k in range(0, n, 8):
                    size = min(8, n - k)
                    out[h, base + k:base + k + size] = buf[h, pl.ds(8 + row + k * R, size, stride=R)]

    start(late[2], late[3])

    scale = 0.5 * time_step
    row_r = lax.broadcasted_iota(jnp.int32, (R, LANES), 0)
    m = [ext[MASK, h, TOP:TOP + R] for h in range(2)]
    m_east, m_west = east_of(m, last_r), west_of(m, first_r)
    j = (row_r + lat * R).astype(jnp.float32)
    planet = coriolis * (2.0 * (j + 0.5) / (R * lat_n) - 1.0)
    for h in range(2):
        fe, fw = m[h] * m_east[h], m[h] * m_west[h]
        if h == 1:
            fe = jnp.where(last_r, 0.0, fe)
        else:
            fw = jnp.where(first_r, 0.0, fw)
        fn = jnp.where(row_r == R - 1, 0.0, m[h] * pltpu.roll(m[h], R - 1, 0))
        fs = jnp.where(row_r == 0, 0.0, m[h] * pltpu.roll(m[h], 1, 0))
        fe, fw, fn, fs = scale * fe, scale * fw, scale * fn, scale * fs
        closed = ((fe + fw) + (fn + fs))
        for i, value in enumerate((fe, fw, fn, fs, m[h] - closed, time_step * planet * m[h],
                                   fe - fw, fn - fs, 1.0 - closed)):
            cf[i, h] = value

    lane_8 = lanes_of(8)
    first, last = lane_8 == 0, lane_8 == LANES - 1

    def level(k, carry):
        at_u = pl.multiple_of(k * R, R)
        at_v = pl.multiple_of((L + k) * R, R)

        def views(buf, at):
            return [buf.at[h, pl.ds(at, R + 16)] for h in range(2)]

        uv, vv = views(vb, at_u), views(vb, at_v)
        tv, sv = views(tb, at_u), views(tb, at_v)
        pv = views(pb, at_u)
        for r in range(0, R, 8):
            def get(view, by=0):
                return [view[h][8 + r + by:16 + r + by] for h in range(2)]

            fe, fw, fn, fs, mid_v, fc, fx, fy, mid_t = [
                [cf[i, h, r:r + 8] for h in range(2)] for i in range(9)]
            u, v, p = get(uv), get(vv), get(pv)
            te = [fe[h] - fe[h] * u[h] for h in range(2)]
            tw = [fw[h] + fw[h] * u[h] for h in range(2)]
            tn = [fn[h] - fn[h] * v[h] for h in range(2)]
            ts = [fs[h] + fs[h] * v[h] for h in range(2)]
            tc = [mid_t[h] + (fx[h] * u[h] + fy[h] * v[h]) for h in range(2)]
            for view, at in ((tv, at_u), (sv, at_v)):
                q, qn, qs = get(view), get(view, 1), get(view, -1)
                qe, qw = east_of(q, last), west_of(q, first)
                for h in range(2):
                    to[h, pl.ds(at + r, 8)] = (
                        (te[h] * qe[h] + tw[h] * qw[h]) + (tn[h] * qn[h] + ts[h] * qs[h])) + tc[h] * q[h]
            un, us = get(uv, 1), get(uv, -1)
            less_e = east_of([u[h] - p[h] for h in range(2)], last)
            more_w = west_of([u[h] + p[h] for h in range(2)], first)
            for h in range(2):
                vo[h, pl.ds(at_u + r, 8)] = (
                    ((fe[h] * less_e[h] + fw[h] * more_w[h]) + (fn[h] * un[h] + fs[h] * us[h]))
                    + ((mid_v[h] * u[h] + fx[h] * p[h]) + fc[h] * v[h]))
            vn, vs, pn, ps = get(vv, 1), get(vv, -1), get(pv, 1), get(pv, -1)
            ve, vw = east_of(v, last), west_of(v, first)
            for h in range(2):
                less_n, more_s = vn[h] - pn[h], vs[h] + ps[h]
                vo[h, pl.ds(at_v + r, 8)] = (
                    ((fe[h] * ve[h] + fw[h] * vw[h]) + (fn[h] * less_n + fs[h] * more_s))
                    + ((mid_v[h] * v[h] + fy[h] * p[h]) - fc[h] * u[h]))
        return carry

    def arrived(which):
        for i in which:
            urgent[i].wait_recv()

    from_west, from_east = (0, 4, 2), (1, 5, 3)
    lax.fori_loop(0, MEET, level, 0)

    @pl.when(last_col)
    def _():
        arrived(from_west)
        start(*westward, late[1])

    lax.fori_loop(MEET, L, level, 0)

    keep_s = jnp.where(lat == 0, 0.0, 1.0)
    keep_n = jnp.where(lat == lat_n - 1, 0.0, 1.0)
    low, high = TOP - 8, TOP + R

    def keeps(f):
        return (keep_s, keep_n) if f == MASK else (1.0, 1.0)

    arrived((6, 7))

    @pl.when(jnp.logical_not(east_late))
    def _():
        arrived(from_east)

    @pl.when(east_late & jnp.logical_not(last_col))
    def _():
        arrived(from_west)

    def turn(by):
        return lax.rem(by + 4 * LANES, LANES)

    to_end = side * (LANES - HALO)
    for f in range(5):
        off = HALO * f
        ks, kn = keeps(f)
        for h in range(2):
            ext[f, h, low:low + 8] = got_s[h, 8 * f:8 * f + 8] * ks
            ext[f, h, high:high + 8] = got_n[h, 8 * f:8 * f + 8] * kn
        for part in range(2):
            ext[f, 2, TOP + mid * part:TOP + mid * (part + 1)] = shift(
                got[1 - side], turn(to_end - off - 64 * part))
        ext[f, 2, high:high + 8] = kn * shift(corner[side], turn(to_end - off))
        ext[f, 2, low:low + 8] = ks * shift(corner[2 + side], turn(to_end - off - 64))
    for f, place in far:
        ks, kn = keeps(f)
        for h in range(2):
            ext[f, h, low - 1:low] = got_s[h, 40 + place:41 + place] * ks
            ext[f, h, high + 8:high + 9] = got_n[h, 40 + place:41 + place] * kn

    for f in range(5):
        for r in range(0, R + 2 * TOP, 16):
            strip[f, 0, r:r + 16] = shift(ext[f, side, r:r + 16], 64)

    step = 16
    lane_s = lanes_of(step)
    first_s, last_s = lane_s == 0, lane_s == LANES - 1

    def solve(fld, other, run, coe, n):
        for r in range(0, R + 16, step):
            def near(f, by=0):
                return [fld[f, t, low + r + by:low + r + by + step] for t in range(n)]

            mm, mn, ms = near(MASK), near(MASK, 1), near(MASK, -1)
            me, mw = east_of(mm, last_s), west_of(mm, first_s)
            us, vs, vn, vso = near(USUM), near(VSUM), near(VSUM, 1), near(VSUM, -1)
            ue, uw = east_of(us, last_s), west_of(us, first_s)
            ss, ds = near(SURF), near(DAMP)
            for t in range(n):
                fe, fw, fn, fs = mm[t] * me[t], mm[t] * mw[t], mm[t] * mn[t], mm[t] * ms[t]
                column = 0.5 * ((fe * (ue[t] + us[t]) - fw * (us[t] + uw[t]))
                                + (fn * (vn[t] + vs[t]) - fs * (vs[t] + vso[t])))
                forcing = ds[t] * ss[t] - transport * column
                inv = 1.0 / (ds[t] + fe + fw + fn + fs)
                for i, value in enumerate((forcing, fe, fw, fn, fs)):
                    coe[i, t, r:r + step] = value * inv
        for sweep, (wa, wc) in enumerate(sweep_weights(SWEEPS)):
            even = sweep % 2 == 0

            def rd(t, at):
                return fld[SURF, t, at:at + step] if even else other[t, at:at + step]

            for r in range(0, R + 16, step):
                at = low + r
                x = [rd(t, at) for t in range(n)]
                xe, xw = east_of(x, last_s), west_of(x, first_s)
                for t in range(n):
                    g, ce, cw, cn, cs = [coe[i, t, r:r + step] for i in range(5)]
                    resid = (((g - x[t]) + ce * xe[t])
                             + (cw * xw[t] + cn * rd(t, at + 1))) + cs * rd(t, at - 1)
                    move = wc * resid
                    if sweep > 0:
                        move = move + wa * run[t, r:r + step]
                    run[t, r:r + step] = move
                    if even:
                        other[t, at:at + step] = x[t] + move
                    else:
                        fld[SURF, t, at:at + step] = x[t] + move

    push = 0.5 * time_step * gravity

    def gradient(fld, r, n, wanted):
        def near(f, by=0):
            return [fld[f, t, TOP + r + by:TOP + r + by + step] for t in range(n)]

        mm, mn, ms = near(MASK), near(MASK, 1), near(MASK, -1)
        me, mw = east_of(mm, last_s), west_of(mm, first_s)
        x, xn, xs = near(SURF), near(SURF, 1), near(SURF, -1)
        xe, xw = east_of(x, last_s), west_of(x, first_s)
        for h in range(wanted):
            k = push * mm[h]
            yield (k * (me[h] * (xe[h] - x[h]) + mw[h] * (x[h] - xw[h])),
                   k * (mn[h] * (xn[h] - x[h]) + ms[h] * (x[h] - xs[h])), x[h])

    solve(ext, xb, dd, co, 3)
    for r in range(0, R, step):
        for h, (du, dv, x) in enumerate(gradient(ext, r, 3, 2)):
            cuv[0, h, r:r + step] = du
            cuv[1, h, r:r + step] = dv
            so[h, r:r + step] = x

    late[2].wait_recv()
    late[3].wait_recv()
    for h in range(2):
        mask_n = scale * (ext[MASK, h, TOP + R - 1:TOP + R] * ext[MASK, h, TOP + R:TOP + R + 1])
        mask_s = scale * (ext[MASK, h, TOP:TOP + 1] * ext[MASK, h, TOP - 1:TOP])

        def parts(f):
            return slice(f * L, (f + 1) * L)

        gn = [mask_n * (grow_n[h, parts(f)] - row_n[h, parts(f)]) for f in range(5)]
        gs = [mask_s * (row_s[h, parts(f)] - grow_s[h, parts(f)]) for f in range(5)]
        vn, vs = row_n[h, parts(1)], row_s[h, parts(1)]
        fix_n = (gn[0], gn[1] - gn[4], gn[2] * (1.0 - vn), gn[3] * (1.0 - vn))
        fix_s = (-gs[0], -(gs[1] + gs[4]), -gs[2] * (1.0 + vs), -gs[3] * (1.0 + vs))
        for f in range(4):
            out, c = (vo, f) if f < 2 else (to, f - 2)
            for part, row in ((fix_n[f], R - 1), (fix_s[f], 0)):
                for k in range(0, L, 8):
                    size = min(8, L - k)
                    at = pl.ds((c * L + k) * R + row, size, stride=R)
                    out[h, at] = out[h, at] + part[k:k + size]

    def beside(own):
        return jnp.where(lane_r < 3 * L, shift(own, 2 * L), shift(own, 3 * L))

    def choose(u_part, v_part, t_part):
        return jnp.where(lane_r < L, u_part, jnp.where(lane_r < 2 * L, v_part, t_part))

    def beyond(from_where, lane):
        pair = [got[from_where][:, at:at + 1] for at in (lane, lane + 64)]
        return jnp.concatenate(pair, axis=0)

    def fix_east():
        late[1].wait_recv()
        open_e = ext[MASK, 1, TOP:TOP + R][:, LANES - 1:] * beyond(1, HALO * MASK)
        own_e = shift(col_e[...], 1)
        g_e = (scale * open_e) * (gcol_e[...] - own_e)
        fix[0] = shift(choose(g_e - shift(g_e, -4 * L), g_e, g_e * (1.0 - beside(own_e))), -1)

    def fix_west():
        late[0].wait_recv()
        open_w = ext[MASK, 0, TOP:TOP + R][:, :1] * beyond(0, HALO * MASK + HALO - 1)
        own_w = col_w[...]
        g_w = (scale * open_w) * (own_w - shift(gcol_w[...], 1))
        fix[1] = -choose(g_w + shift(g_w, -4 * L), g_w, g_w * (1.0 + beside(own_w)))

    pl.when(jnp.logical_not(east_late))(fix_east)
    pl.when(east_late)(fix_west)

    @pl.when(first_col)
    def _():
        pl.semaphore_wait(hello, 3)
        start(*westward, late[1])

    @pl.when(jnp.logical_not(east_late))
    def _():
        arrived(from_west)

    @pl.when(east_late)
    def _():
        arrived(from_east)

    halo_m = lax.shift_right_logical(lane_m, 6) == side
    halo_8 = lax.shift_right_logical(lane_8, 6) == side
    for f in range(5):
        to_halo = 64 - HALO + HALO * side - HALO * f
        ks, kn = keeps(f)
        for part in range(2):
            here = slice(TOP + mid * part, TOP + mid * (part + 1))
            strip[f, 0, here] = jnp.where(
                halo_m, shift(got[side], turn(to_halo - 64 * part)), strip[f, 0, here])
        here = slice(high, high + 8)
        strip[f, 0, here] = jnp.where(
            halo_8, kn * shift(corner[1 - side], turn(to_halo)), strip[f, 0, here])
        here = slice(low, low + 8)
        strip[f, 0, here] = jnp.where(
            halo_8, ks * shift(corner[3 - side], turn(to_halo - 64)), strip[f, 0, here])
    solve(strip, sxb, sdd, sco, 1)
    edge = lax.shift_right_logical(lane_s, 5) == 3 * side
    for r in range(0, R, step):
        du, dv, x = next(gradient(strip, r, 1, 1))
        here = slice(r, r + step)
        cuv[0, side, here] = jnp.where(edge, shift(du, 64), cuv[0, side, here])
        cuv[1, side, here] = jnp.where(edge, shift(dv, 64), cuv[1, side, here])
        so[side, here] = jnp.where(edge, shift(x, 64), so[side, here])

    pl.when(jnp.logical_not(east_late))(fix_west)
    pl.when(east_late)(fix_east)

    for copy in urgent + late:
        copy.wait_send()


def write_kernel(
    levels, rows, vo, to, cuv, so, fix, vel_next, tra_next, srf_next, vbuf, tbuf, sem,
):
    L, R = levels, rows
    copies = []

    def put(src, dst):
        copy = pltpu.make_async_copy(src, dst, sem.at[len(copies)])
        copy.start()
        copies.append(copy)

    def half(h):
        return pl.ds(h * LANES, LANES)

    for h in range(2):
        put(so.at[h], srf_next.at[:, half(h)])
    lane_r = lanes_of(R)
    first_r, last_r = lane_r == 0, lane_r == LANES - 1
    chunk = L // PIECES
    for f in (2, 3, 0, 1):
        c = f % 2
        src, buf, out = (vo, vbuf, vel_next) if f < 2 else (to, tbuf, tra_next)
        for k0 in range(0, L, chunk):
            for k in range(k0, k0 + chunk):
                at = (c * L + k) * R
                lane = f * L + k
                edge = shift(jnp.where(lane_r == lane, fix[1], fix[0]), -lane)
                for h in range(2):
                    value = src[h, at:at + R]
                    if f < 2:
                        value = value - cuv[c, h]
                    buf[at:at + R, h * LANES:(h + 1) * LANES] = jnp.where(
                        last_r if h else first_r, value + edge, value)
            here = pl.ds((c * L + k0) * R, chunk * R)
            put(buf.at[here], out.at[here])
    for copy in copies:
        copy.wait()


def shards(lat_n, lon_n, velocity, tracer, surface, damping, ocean):
    _, L, R, C = velocity.shape
    f32 = jnp.float32
    anywhere = pl.BlockSpec(memory_space=pl.ANY)
    inside = pl.BlockSpec(memory_space=pltpu.VMEM)

    def scratch(*shape):
        return pltpu.VMEM(shape, f32)

    flat = 2 * L * R
    ring = R + 2 * TOP
    mid = [
        pltpu.VMEM((2, flat, LANES), f32),
        pltpu.VMEM((2, flat, LANES), f32),
        pltpu.VMEM((2, 2, R, LANES), f32),
        pltpu.VMEM((2, R, LANES), f32),
        pltpu.VMEM((2, R, LANES), f32),
    ]
    packed = 5 * L // 8 * 8 + 8
    made = pl.pallas_call(
        functools.partial(step_kernel, L, R, lat_n, lon_n),
        out_shape=mid,
        in_specs=[anywhere] * 6,
        out_specs=[inside] * 5,
        scratch_shapes=[
            scratch(2, flat + 16, LANES), scratch(2, flat + 16, LANES), scratch(2, L * R + 16, LANES),
            pltpu.VMEM((2, R, LANES), jnp.int32),
            scratch(5, 3, ring, LANES), scratch(3, ring, LANES), scratch(3, R + 16, LANES),
            scratch(5, 3, R + 16, LANES), scratch(9, 2, R, LANES),
            scratch(5, 1, ring, LANES), scratch(1, ring, LANES), scratch(1, R + 16, LANES),
            scratch(5, 1, R + 16, LANES),
            scratch(R // 2, LANES), scratch(R // 2, LANES), scratch(2, R // 2, LANES),
            scratch(4, 8, LANES), scratch(2, 2 * L, 8, LANES), scratch(2, 8, LANES),
            scratch(2, 48, LANES), scratch(2, 48, LANES), scratch(2, 48, LANES), scratch(2, 48, LANES),
            scratch(R, LANES), scratch(R, LANES), scratch(R, LANES), scratch(R, LANES),
            scratch(2, packed, LANES), scratch(2, packed, LANES),
            scratch(2, packed, LANES), scratch(2, packed, LANES),
            pltpu.SemaphoreType.DMA((14,)),
            pltpu.SemaphoreType.DMA((12,)),
            pltpu.SemaphoreType.DMA((12,)),
            pltpu.SemaphoreType.REGULAR,
        ],
        compiler_params=pltpu.CompilerParams(
            collective_id=0, has_side_effects=True, vmem_limit_bytes=32 * 1024 * 1024),
        name="ocean_step",
    )(*[
        pltpu.with_memory_space_constraint(x, pltpu.HBM)
        for x in (velocity.reshape(flat, C), tracer.reshape(flat, C), surface, damping, ocean,
                  velocity.reshape(2 * L, R, C))
    ])
    vel_next, tra_next, srf_next = pl.pallas_call(
        functools.partial(write_kernel, L, R),
        out_shape=[
            jax.ShapeDtypeStruct((flat, C), f32),
            jax.ShapeDtypeStruct((flat, C), f32),
            jax.ShapeDtypeStruct((R, C), f32),
        ],
        in_specs=[inside] * 5,
        out_specs=[anywhere] * 3,
        scratch_shapes=[scratch(flat, C), scratch(flat, C), pltpu.SemaphoreType.DMA((2 + 4 * PIECES,))],
        compiler_params=pltpu.CompilerParams(vmem_limit_bytes=32 * 1024 * 1024),
        name="ocean_write",
    )(*made)
    return vel_next.reshape(velocity.shape), tra_next.reshape(tracer.shape), srf_next


def solution(mesh):
    placed = (
        P(None, None, "lat", "lon"),
        P(None, None, "lat", "lon"),
        P("lat", "lon"),
        P("lat", "lon"),
        P("lat", "lon"),
    )
    return jax.shard_map(
        functools.partial(shards, mesh.shape["lat"], mesh.shape["lon"]),
        mesh=mesh,
        in_specs=placed,
        out_specs=(P(None, None, "lat", "lon"), P(None, None, "lat", "lon"), P("lat", "lon")),
        check_vma=False,
    )
```

```python
import functools

import jax
import jax.numpy as jnp
from jax import lax
from jax.experimental import pallas as pl
from jax.experimental.pallas import tpu as pltpu
from jax.sharding import PartitionSpec as P

SWEEPS = 8

time_step = 0.2
gravity = 4.0
coriolis = 1.0
viscosity = 0.5
diffusivity = 0.5
thermal = 0.2
haline = 0.15
buoyancy = 2.0
transport = 1.0
damping_floor = 0.01

LANES = 128
PIECES = 2
MEET = 15
HALO = 9
TOP = 16
MESH = pl.DeviceIdType.MESH
SURF, MASK, DAMP, USUM, VSUM = range(5)


def sweep_weights(count):
    low = damping_floor / (damping_floor + 4.0)
    high = 2.0 - low
    theta = (high + low) / 2.0
    delta = (high - low) / 2.0
    sigma = theta / delta
    weights = [(0.0, 1.0 / theta)]
    rho_now = 1.0 / sigma
    for _ in range(count - 1):
        rho_new = 1.0 / (2.0 * sigma - rho_now)
        weights.append((rho_new * rho_now, 2.0 * rho_new / delta))
        rho_now = rho_new
    return weights


def lanes_of(rows):
    return lax.broadcasted_iota(jnp.int32, (rows, LANES), 1)


def shift(x, by):
    if isinstance(by, int):
        by %= LANES
        if by == 0:
            return x
    return pltpu.roll(x, by, 1)


def east_of(q, last):
    r = [shift(x, -1) for x in q]
    n = len(q)
    if n == 1:
        return r
    return [jnp.where(last, r[(i + 1) % n], r[i]) for i in range(n)]


def west_of(q, first):
    r = [shift(x, 1) for x in q]
    n = len(q)
    if n == 1:
        return r
    return [jnp.where(first, r[(i - 1) % n], r[i]) for i in range(n)]


def step_kernel(
    levels, rows, lat_n, lon_n,
    vel, tra, srf, dmp, ocn, vel_levels,
    vo, to, cuv, so, fix,
    vb, tb, pb, oc, ext, xb, dd, co, cf, strip, sxb, sdd, sco,
    msg_e, msg_w, got, corner, ends, msg_c,
    msg_n, msg_s, got_n, got_s,
    col_e, col_w, gcol_e, gcol_w,
    row_n, row_s, grow_n, grow_s,
    local_sem, send_sem, recv_sem, hello,
):
    L, R = levels, rows
    lat, lon = lax.axis_index("lat"), lax.axis_index("lon")
    north, south = lax.rem(lat + 1, lat_n), lax.rem(lat + lat_n - 1, lat_n)
    east, west = lax.rem(lon + 1, lon_n), lax.rem(lon + lon_n - 1, lon_n)

    barrier = pltpu.get_barrier_semaphore()

    first_col, last_col = lon == 0, lon == lon_n - 1
    few = first_col | last_col
    east_late = lon >= lon_n - 2
    side = jnp.where(east_late, 1, 0)

    def greet(*peers):
        for peer in peers:
            pl.semaphore_signal(barrier, inc=1, device_id=peer, device_id_type=MESH)

    greet((north, west), (south, west), (lat, west))

    @pl.when(jnp.logical_not(east_late))
    def _():
        greet((north, east), (south, east), (lat, east))

    greet((north, lon), (south, lon))

    count = [0]

    def fetch(src, dst):
        copy = pltpu.make_async_copy(src, dst, local_sem.at[count[0]])
        count[0] += 1
        copy.start()
        return copy

    def half(h):
        return pl.ds(h * LANES, LANES)

    inner = pl.ds(TOP, R)
    vel_copies, small = {}, {}
    for h in (1, 0):
        small[h] = [
            fetch(ocn.at[:, half(h)], oc.at[h]),
            fetch(srf.at[:, half(h)], ext.at[SURF, h, inner]),
            fetch(dmp.at[:, half(h)], ext.at[DAMP, h, inner]),
        ]
        if h == 1:
            end_copies = [
                fetch(vel_levels.at[:, pl.ds(e * (R - 8), 8), half(1)], ends.at[e]) for e in range(2)]
        for c in range(2):
            here = pl.ds(c * L * R, L * R)
            vel_copies[c, h] = fetch(vel.at[here, half(h)], vb.at[h, pl.ds(8 + c * L * R, L * R)])
    tra_copies = [fetch(tra.at[:, half(h)], tb.at[h, pl.ds(8, 2 * L * R)]) for h in range(2)]

    @pl.when(last_col)
    def _():
        pl.semaphore_wait(barrier, 5)
        for peer in ((north, east), (south, east), (lat, east)):
            pl.semaphore_signal(hello, inc=1, device_id=peer, device_id_type=MESH)

    zero8 = jnp.zeros((8, LANES), jnp.float32)
    for h in range(2):
        for buf, size in ((vb, 2 * L * R), (tb, 2 * L * R), (pb, L * R)):
            buf[h, 0:8] = zero8
            buf[h, 8 + size:16 + size] = zero8

    mid = R // 2
    lane_m = lanes_of(mid)
    thick = [2.0 * (k + 1.0) / (L * (L + 1)) for k in range(L)]

    def pack_cols(h, field, acc):
        off = HALO * field
        for part in range(2):
            at = off + 64 * part
            keep = (lane_m >= at) & (lane_m < at + HALO)
            rows_here = slice(TOP + mid * part, TOP + mid * (part + 1))
            acc = jnp.where(keep, shift(ext[field, h, rows_here], at + h * HALO), acc)
        return acc

    def take_small(h):
        for copy in small[h]:
            copy.wait()
        ext[MASK, h, TOP:TOP + R] = oc[h].astype(jnp.float32)

    def urgent_half(h, out):
        if h == 0:
            take_small(0)
        acc = jnp.zeros((mid, LANES), jnp.float32)
        for field in (SURF, MASK, DAMP):
            acc = pack_cols(h, field, acc)
        for c in range(2):
            vel_copies[c, h].wait()
            total = None
            for k in range(L):
                at = 8 + (c * L + k) * R
                term = thick[k] * vb[h, at:at + R]
                total = term if total is None else total + term
            ext[USUM + c, h, TOP:TOP + R] = total
            acc = pack_cols(h, USUM + c, acc)
        out[...] = acc

    far = ((SURF, 0), (MASK, 1), (VSUM, 2))

    def remote(i, src, dst, peer):
        return pltpu.make_async_remote_copy(
            src_ref=src, dst_ref=dst, send_sem=send_sem.at[i], recv_sem=recv_sem.at[i],
            device_id=peer, device_id_type=MESH)

    urgent = [
        remote(0, msg_e, got.at[0], (lat, east)),
        remote(1, msg_w, got.at[1], (lat, west)),
        remote(2, msg_c.at[1], corner.at[3], (north, east)),
        remote(3, msg_w.at[pl.ds(mid - 8, 8)], corner.at[2], (north, west)),
        remote(4, msg_c.at[0], corner.at[1], (south, east)),
        remote(5, msg_w.at[pl.ds(0, 8)], corner.at[0], (south, west)),
        remote(6, msg_n, got_s, (north, lon)),
        remote(7, msg_s, got_n, (south, lon)),
    ]
    late = [
        remote(8, col_e, gcol_w, (lat, east)),
        remote(9, col_w, gcol_e, (lat, west)),
        remote(10, row_n, grow_s, (north, lon)),
        remote(11, row_s, grow_n, (south, lon)),
    ]

    westward = [urgent[3], urgent[5], urgent[1]]

    def start(*copies):
        for copy in copies:
            copy.start()

    take_small(1)
    lane_8 = lanes_of(8)
    for e in range(2):
        end_copies[e].wait()
        here = slice(TOP + e * (R - 8), TOP + e * (R - 8) + 8)
        fields = [ext[f, 1, here] for f in (SURF, MASK, DAMP)]
        for c in range(2):
            total = None
            for k in range(L):
                term = thick[k] * ends[e, c * L + k]
                total = term if total is None else total + term
            fields.append(total)
        acc = jnp.zeros((8, LANES), jnp.float32)
        for f, value in enumerate(fields):
            at = HALO * f + 64 * e
            acc = jnp.where((lane_8 >= at) & (lane_8 < at + HALO), shift(value, at + HALO), acc)
        msg_c[e] = acc

    @pl.when(last_col)
    def _():
        start(urgent[2], urgent[4])

    urgent_half(1, msg_e)

    @pl.when(first_col)
    def _():
        pl.semaphore_wait(barrier, 5)

    @pl.when(jnp.logical_not(few))
    def _():
        pl.semaphore_wait(barrier, 8)

    @pl.when(jnp.logical_not(last_col))
    def _():
        start(urgent[2], urgent[4])

    start(urgent[0])
    urgent_half(0, msg_w)

    @pl.when(jnp.logical_not(few))
    def _():
        start(*westward)

    for h in range(2):
        for field in range(5):
            msg_n[h, 8 * field:8 * field + 8] = ext[field, h, TOP + R - 8:TOP + R]
            msg_s[h, 8 * field:8 * field + 8] = ext[field, h, TOP:TOP + 8]
        msg_n[h, 40:48] = zero8
        msg_s[h, 40:48] = zero8
        for field, place in far:
            msg_n[h, 40 + place:41 + place] = ext[field, h, TOP + R - 9:TOP + R - 8]
            msg_s[h, 40 + place:41 + place] = ext[field, h, TOP + 8:TOP + 9]
    start(urgent[6], urgent[7])

    for copy in tra_copies:
        copy.wait()
    for h in range(2):
        press = None
        for k in range(L):
            at = 8 + k * R
            warm = (buoyancy * thermal * thick[k]) * tb[h, at:at + R]
            salt = (buoyancy * haline * thick[k]) * tb[h, at + L * R:at + L * R + R]
            press = warm - salt if press is None else press + (warm - salt)
            pb[h, at:at + R] = press

    stacks = ((vb, 0), (vb, 1), (tb, 0), (tb, 1), (pb, 0))
    lane_r = lanes_of(R)
    first_r, last_r = lane_r == 0, lane_r == LANES - 1
    acc_w = acc_e = jnp.zeros((R, LANES), jnp.float32)
    for f, (buf, c) in enumerate(stacks):
        for k in range(L):
            at = 8 + (c * L + k) * R
            lane = f * L + k
            both = shift(jnp.where(last_r, buf[1, at:at + R], buf[0, at:at + R]), lane)
            acc_w = jnp.where(lane_r == lane, both, acc_w)
            acc_e = jnp.where(lane_r == (lane - 1) % LANES, both, acc_e)
    col_w[...], col_e[...] = acc_w, acc_e

    late[0].start()

    @pl.when(jnp.logical_not(few))
    def _():
        late[1].start()

    for h in range(2):
        for out, row in ((row_n, R - 1), (row_s, 0)):
            out[h, 5 * L // 8 * 8:] = zero8
            for buf, base, n in ((vb, 0, 2 * L), (tb, 2 * L, 2 * L), (pb, 4 * L, L)):
                for k in range(0, n, 8):
                    size = min(8, n - k)
                    out[h, base + k:base + k + size] = buf[h, pl.ds(8 + row + k * R, size, stride=R)]

    start(late[2], late[3])

    scale = 0.5 * time_step
    row_r = lax.broadcasted_iota(jnp.int32, (R, LANES), 0)
    m = [ext[MASK, h, TOP:TOP + R] for h in range(2)]
    m_east, m_west = east_of(m, last_r), west_of(m, first_r)
    j = (row_r + lat * R).astype(jnp.float32)
    planet = coriolis * (2.0 * (j + 0.5) / (R * lat_n) - 1.0)
    for h in range(2):
        fe, fw = m[h] * m_east[h], m[h] * m_west[h]
        if h == 1:
            fe = jnp.where(last_r, 0.0, fe)
        else:
            fw = jnp.where(first_r, 0.0, fw)
        fn = jnp.where(row_r == R - 1, 0.0, m[h] * pltpu.roll(m[h], R - 1, 0))
        fs = jnp.where(row_r == 0, 0.0, m[h] * pltpu.roll(m[h], 1, 0))
        fe, fw, fn, fs = scale * fe, scale * fw, scale * fn, scale * fs
        closed = ((fe + fw) + (fn + fs))
        for i, value in enumerate((fe, fw, fn, fs, m[h] - closed, time_step * planet * m[h],
                                   fe - fw, fn - fs, 1.0 - closed)):
            cf[i, h] = value

    lane_8 = lanes_of(8)
    first, last = lane_8 == 0, lane_8 == LANES - 1

    def level(k, carry):
        at_u = pl.multiple_of(k * R, R)
        at_v = pl.multiple_of((L + k) * R, R)

        def views(buf, at):
            return [buf.at[h, pl.ds(at, R + 16)] for h in range(2)]

        uv, vv = views(vb, at_u), views(vb, at_v)
        tv, sv = views(tb, at_u), views(tb, at_v)
        pv = views(pb, at_u)
        for r in range(0, R, 8):
            def get(view, by=0):
                return [view[h][8 + r + by:16 + r + by] for h in range(2)]

            fe, fw, fn, fs, mid_v, fc, fx, fy, mid_t = [
                [cf[i, h, r:r + 8] for h in range(2)] for i in range(9)]
            u, v, p = get(uv), get(vv), get(pv)
            te = [fe[h] - fe[h] * u[h] for h in range(2)]
            tw = [fw[h] + fw[h] * u[h] for h in range(2)]
            tn = [fn[h] - fn[h] * v[h] for h in range(2)]
            ts = [fs[h] + fs[h] * v[h] for h in range(2)]
            tc = [mid_t[h] + (fx[h] * u[h] + fy[h] * v[h]) for h in range(2)]
            for view, at in ((tv, at_u), (sv, at_v)):
                q, qn, qs = get(view), get(view, 1), get(view, -1)
                qe, qw = east_of(q, last), west_of(q, first)
                for h in range(2):
                    to[h, pl.ds(at + r, 8)] = (
                        (te[h] * qe[h] + tw[h] * qw[h]) + (tn[h] * qn[h] + ts[h] * qs[h])) + tc[h] * q[h]
            un, us = get(uv, 1), get(uv, -1)
            less_e = east_of([u[h] - p[h] for h in range(2)], last)
            more_w = west_of([u[h] + p[h] for h in range(2)], first)
            for h in range(2):
                vo[h, pl.ds(at_u + r, 8)] = (
                    ((fe[h] * less_e[h] + fw[h] * more_w[h]) + (fn[h] * un[h] + fs[h] * us[h]))
                    + ((mid_v[h] * u[h] + fx[h] * p[h]) + fc[h] * v[h]))
            vn, vs, pn, ps = get(vv, 1), get(vv, -1), get(pv, 1), get(pv, -1)
            ve, vw = east_of(v, last), west_of(v, first)
            for h in range(2):
                less_n, more_s = vn[h] - pn[h], vs[h] + ps[h]
                vo[h, pl.ds(at_v + r, 8)] = (
                    ((fe[h] * ve[h] + fw[h] * vw[h]) + (fn[h] * less_n + fs[h] * more_s))
                    + ((mid_v[h] * v[h] + fy[h] * p[h]) - fc[h] * u[h]))
        return carry

    def arrived(which):
        for i in which:
            urgent[i].wait_recv()

    from_west, from_east = (0, 4, 2), (1, 5, 3)
    lax.fori_loop(0, MEET, level, 0)

    @pl.when(last_col)
    def _():
        arrived(from_west)
        start(*westward, late[1])

    lax.fori_loop(MEET, L, level, 0)

    keep_s = jnp.where(lat == 0, 0.0, 1.0)
    keep_n = jnp.where(lat == lat_n - 1, 0.0, 1.0)
    low, high = TOP - 8, TOP + R

    def keeps(f):
        return (keep_s, keep_n) if f == MASK else (1.0, 1.0)

    arrived((6, 7))

    @pl.when(jnp.logical_not(east_late))
    def _():
        arrived(from_east)

    @pl.when(east_late & jnp.logical_not(last_col))
    def _():
        arrived(from_west)

    def turn(by):
        return lax.rem(by + 4 * LANES, LANES)

    to_end = side * (LANES - HALO)
    for f in range(5):
        off = HALO * f
        ks, kn = keeps(f)
        for h in range(2):
            ext[f, h, low:low + 8] = got_s[h, 8 * f:8 * f + 8] * ks
            ext[f, h, high:high + 8] = got_n[h, 8 * f:8 * f + 8] * kn
        for part in range(2):
            ext[f, 2, TOP + mid * part:TOP + mid * (part + 1)] = shift(
                got[1 - side], turn(to_end - off - 64 * part))
        ext[f, 2, high:high + 8] = kn * shift(corner[side], turn(to_end - off))
        ext[f, 2, low:low + 8] = ks * shift(corner[2 + side], turn(to_end - off - 64))
    for f, place in far:
        ks, kn = keeps(f)
        for h in range(2):
            ext[f, h, low - 1:low] = got_s[h, 40 + place:41 + place] * ks
            ext[f, h, high + 8:high + 9] = got_n[h, 40 + place:41 + place] * kn

    for f in range(5):
        for r in range(0, R + 2 * TOP, 16):
            strip[f, 0, r:r + 16] = shift(ext[f, side, r:r + 16], 64)

    step = 16
    lane_s = lanes_of(step)
    first_s, last_s = lane_s == 0, lane_s == LANES - 1

    def solve(fld, other, run, coe, n):
        for r in range(0, R + 16, step):
            def near(f, by=0):
                return [fld[f, t, low + r + by:low + r + by + step] for t in range(n)]

            mm, mn, ms = near(MASK), near(MASK, 1), near(MASK, -1)
            me, mw = east_of(mm, last_s), west_of(mm, first_s)
            us, vs, vn, vso = near(USUM), near(VSUM), near(VSUM, 1), near(VSUM, -1)
            ue, uw = east_of(us, last_s), west_of(us, first_s)
            ss, ds = near(SURF), near(DAMP)
            for t in range(n):
                fe, fw, fn, fs = mm[t] * me[t], mm[t] * mw[t], mm[t] * mn[t], mm[t] * ms[t]
                column = 0.5 * ((fe * (ue[t] + us[t]) - fw * (us[t] + uw[t]))
                                + (fn * (vn[t] + vs[t]) - fs * (vs[t] + vso[t])))
                forcing = ds[t] * ss[t] - transport * column
                inv = 1.0 / (ds[t] + fe + fw + fn + fs)
                for i, value in enumerate((forcing, fe, fw, fn, fs)):
                    coe[i, t, r:r + step] = value * inv
        for sweep, (wa, wc) in enumerate(sweep_weights(SWEEPS)):
            even = sweep % 2 == 0

            def rd(t, at):
                return fld[SURF, t, at:at + step] if even else other[t, at:at + step]

            for r in range(0, R + 16, step):
                at = low + r
                x = [rd(t, at) for t in range(n)]
                xe, xw = east_of(x, last_s), west_of(x, first_s)
                for t in range(n):
                    g, ce, cw, cn, cs = [coe[i, t, r:r + step] for i in range(5)]
                    still = wc * (g - x[t])
                    if sweep > 0:
                        still = still + wa * run[t, r:r + step]
                    if n == 1:
                        move = still + (((wc * ce) * xe[t] + (wc * cw) * xw[t])
                                        + ((wc * cn) * rd(t, at + 1) + (wc * cs) * rd(t, at - 1)))
                    else:
                        move = still + wc * ((ce * xe[t] + cw * xw[t])
                                             + (cn * rd(t, at + 1) + cs * rd(t, at - 1)))
                    run[t, r:r + step] = move
                    if even:
                        other[t, at:at + step] = x[t] + move
                    else:
                        fld[SURF, t, at:at + step] = x[t] + move

    push = 0.5 * time_step * gravity

    def gradient(fld, r, n, wanted):
        def near(f, by=0):
            return [fld[f, t, TOP + r + by:TOP + r + by + step] for t in range(n)]

        mm, mn, ms = near(MASK), near(MASK, 1), near(MASK, -1)
        me, mw = east_of(mm, last_s), west_of(mm, first_s)
        x, xn, xs = near(SURF), near(SURF, 1), near(SURF, -1)
        xe, xw = east_of(x, last_s), west_of(x, first_s)
        for h in range(wanted):
            k = push * mm[h]
            yield (k * (me[h] * (xe[h] - x[h]) + mw[h] * (x[h] - xw[h])),
                   k * (mn[h] * (xn[h] - x[h]) + ms[h] * (x[h] - xs[h])), x[h])

    solve(ext, xb, dd, co, 3)
    for r in range(0, R, step):
        for h, (du, dv, x) in enumerate(gradient(ext, r, 3, 2)):
            cuv[0, h, r:r + step] = du
            cuv[1, h, r:r + step] = dv
            so[h, r:r + step] = x

    late[2].wait_recv()
    late[3].wait_recv()
    for h in range(2):
        mask_n = scale * (ext[MASK, h, TOP + R - 1:TOP + R] * ext[MASK, h, TOP + R:TOP + R + 1])
        mask_s = scale * (ext[MASK, h, TOP:TOP + 1] * ext[MASK, h, TOP - 1:TOP])

        def parts(f):
            return slice(f * L, (f + 1) * L)

        gn = [mask_n * (grow_n[h, parts(f)] - row_n[h, parts(f)]) for f in range(5)]
        gs = [mask_s * (row_s[h, parts(f)] - grow_s[h, parts(f)]) for f in range(5)]
        vn, vs = row_n[h, parts(1)], row_s[h, parts(1)]
        fix_n = (gn[0], gn[1] - gn[4], gn[2] * (1.0 - vn), gn[3] * (1.0 - vn))
        fix_s = (-gs[0], -(gs[1] + gs[4]), -gs[2] * (1.0 + vs), -gs[3] * (1.0 + vs))
        for f in range(4):
            out, c = (vo, f) if f < 2 else (to, f - 2)
            for part, row in ((fix_n[f], R - 1), (fix_s[f], 0)):
                for k in range(0, L, 8):
                    size = min(8, L - k)
                    at = pl.ds((c * L + k) * R + row, size, stride=R)
                    out[h, at] = out[h, at] + part[k:k + size]

    def beside(own):
        return jnp.where(lane_r < 3 * L, shift(own, 2 * L), shift(own, 3 * L))

    def choose(u_part, v_part, t_part):
        return jnp.where(lane_r < L, u_part, jnp.where(lane_r < 2 * L, v_part, t_part))

    def beyond(from_where, lane):
        pair = [got[from_where][:, at:at + 1] for at in (lane, lane + 64)]
        return jnp.concatenate(pair, axis=0)

    def fix_east():
        late[1].wait_recv()
        open_e = ext[MASK, 1, TOP:TOP + R][:, LANES - 1:] * beyond(1, HALO * MASK)
        own_e = shift(col_e[...], 1)
        g_e = (scale * open_e) * (gcol_e[...] - own_e)
        fix[0] = shift(choose(g_e - shift(g_e, -4 * L), g_e, g_e * (1.0 - beside(own_e))), -1)

    def fix_west():
        late[0].wait_recv()
        open_w = ext[MASK, 0, TOP:TOP + R][:, :1] * beyond(0, HALO * MASK + HALO - 1)
        own_w = col_w[...]
        g_w = (scale * open_w) * (own_w - shift(gcol_w[...], 1))
        fix[1] = -choose(g_w + shift(g_w, -4 * L), g_w, g_w * (1.0 + beside(own_w)))

    pl.when(jnp.logical_not(east_late))(fix_east)
    pl.when(east_late)(fix_west)

    @pl.when(first_col)
    def _():
        pl.semaphore_wait(hello, 3)
        start(*westward, late[1])

    @pl.when(jnp.logical_not(east_late))
    def _():
        arrived(from_west)

    @pl.when(east_late)
    def _():
        arrived(from_east)

    halo_m = lax.shift_right_logical(lane_m, 6) == side
    halo_8 = lax.shift_right_logical(lane_8, 6) == side
    for f in range(5):
        to_halo = 64 - HALO + HALO * side - HALO * f
        ks, kn = keeps(f)
        for part in range(2):
            here = slice(TOP + mid * part, TOP + mid * (part + 1))
            strip[f, 0, here] = jnp.where(
                halo_m, shift(got[side], turn(to_halo - 64 * part)), strip[f, 0, here])
        here = slice(high, high + 8)
        strip[f, 0, here] = jnp.where(
            halo_8, kn * shift(corner[1 - side], turn(to_halo)), strip[f, 0, here])
        here = slice(low, low + 8)
        strip[f, 0, here] = jnp.where(
            halo_8, ks * shift(corner[3 - side], turn(to_halo - 64)), strip[f, 0, here])
    solve(strip, sxb, sdd, sco, 1)
    edge = lax.shift_right_logical(lane_s, 5) == 3 * side
    for r in range(0, R, step):
        du, dv, x = next(gradient(strip, r, 1, 1))
        here = slice(r, r + step)
        cuv[0, side, here] = jnp.where(edge, shift(du, 64), cuv[0, side, here])
        cuv[1, side, here] = jnp.where(edge, shift(dv, 64), cuv[1, side, here])
        so[side, here] = jnp.where(edge, shift(x, 64), so[side, here])

    pl.when(jnp.logical_not(east_late))(fix_west)
    pl.when(east_late)(fix_east)

    for copy in urgent + late:
        copy.wait_send()


def write_kernel(
    levels, rows, vo, to, cuv, so, fix, vel_next, tra_next, srf_next, vbuf, tbuf, sem,
):
    L, R = levels, rows
    copies = []

    def put(src, dst):
        copy = pltpu.make_async_copy(src, dst, sem.at[len(copies)])
        copy.start()
        copies.append(copy)

    def half(h):
        return pl.ds(h * LANES, LANES)

    for h in range(2):
        put(so.at[h], srf_next.at[:, half(h)])
    lane_r = lanes_of(R)
    first_r, last_r = lane_r == 0, lane_r == LANES - 1
    chunk = L // PIECES
    for f in (2, 3, 0, 1):
        c = f % 2
        src, buf, out = (vo, vbuf, vel_next) if f < 2 else (to, tbuf, tra_next)
        for k0 in range(0, L, chunk):
            for k in range(k0, k0 + chunk):
                at = (c * L + k) * R
                lane = f * L + k
                edge = shift(jnp.where(lane_r == lane, fix[1], fix[0]), -lane)
                for h in range(2):
                    value = src[h, at:at + R]
                    if f < 2:
                        value = value - cuv[c, h]
                    buf[at:at + R, h * LANES:(h + 1) * LANES] = jnp.where(
                        last_r if h else first_r, value + edge, value)
            here = pl.ds((c * L + k0) * R, chunk * R)
            put(buf.at[here], out.at[here])
    for copy in copies:
        copy.wait()


def shards(lat_n, lon_n, velocity, tracer, surface, damping, ocean):
    _, L, R, C = velocity.shape
    f32 = jnp.float32
    anywhere = pl.BlockSpec(memory_space=pl.ANY)
    inside = pl.BlockSpec(memory_space=pltpu.VMEM)

    def scratch(*shape):
        return pltpu.VMEM(shape, f32)

    flat = 2 * L * R
    ring = R + 2 * TOP
    mid = [
        pltpu.VMEM((2, flat, LANES), f32),
        pltpu.VMEM((2, flat, LANES), f32),
        pltpu.VMEM((2, 2, R, LANES), f32),
        pltpu.VMEM((2, R, LANES), f32),
        pltpu.VMEM((2, R, LANES), f32),
    ]
    packed = 5 * L // 8 * 8 + 8
    made = pl.pallas_call(
        functools.partial(step_kernel, L, R, lat_n, lon_n),
        out_shape=mid,
        in_specs=[anywhere] * 6,
        out_specs=[inside] * 5,
        scratch_shapes=[
            scratch(2, flat + 16, LANES), scratch(2, flat + 16, LANES), scratch(2, L * R + 16, LANES),
            pltpu.VMEM((2, R, LANES), jnp.int32),
            scratch(5, 3, ring, LANES), scratch(3, ring, LANES), scratch(3, R + 16, LANES),
            scratch(5, 3, R + 16, LANES), scratch(9, 2, R, LANES),
            scratch(5, 1, ring, LANES), scratch(1, ring, LANES), scratch(1, R + 16, LANES),
            scratch(5, 1, R + 16, LANES),
            scratch(R // 2, LANES), scratch(R // 2, LANES), scratch(2, R // 2, LANES),
            scratch(4, 8, LANES), scratch(2, 2 * L, 8, LANES), scratch(2, 8, LANES),
            scratch(2, 48, LANES), scratch(2, 48, LANES), scratch(2, 48, LANES), scratch(2, 48, LANES),
            scratch(R, LANES), scratch(R, LANES), scratch(R, LANES), scratch(R, LANES),
            scratch(2, packed, LANES), scratch(2, packed, LANES),
            scratch(2, packed, LANES), scratch(2, packed, LANES),
            pltpu.SemaphoreType.DMA((14,)),
            pltpu.SemaphoreType.DMA((12,)),
            pltpu.SemaphoreType.DMA((12,)),
            pltpu.SemaphoreType.REGULAR,
        ],
        compiler_params=pltpu.CompilerParams(
            collective_id=0, has_side_effects=True, vmem_limit_bytes=32 * 1024 * 1024),
        name="ocean_step",
    )(*[
        pltpu.with_memory_space_constraint(x, pltpu.HBM)
        for x in (velocity.reshape(flat, C), tracer.reshape(flat, C), surface, damping, ocean,
                  velocity.reshape(2 * L, R, C))
    ])
    vel_next, tra_next, srf_next = pl.pallas_call(
        functools.partial(write_kernel, L, R),
        out_shape=[
            jax.ShapeDtypeStruct((flat, C), f32),
            jax.ShapeDtypeStruct((flat, C), f32),
            jax.ShapeDtypeStruct((R, C), f32),
        ],
        in_specs=[inside] * 5,
        out_specs=[anywhere] * 3,
        scratch_shapes=[scratch(flat, C), scratch(flat, C), pltpu.SemaphoreType.DMA((2 + 4 * PIECES,))],
        compiler_params=pltpu.CompilerParams(vmem_limit_bytes=32 * 1024 * 1024),
        name="ocean_write",
    )(*made)
    return vel_next.reshape(velocity.shape), tra_next.reshape(tracer.shape), srf_next


def solution(mesh):
    placed = (
        P(None, None, "lat", "lon"),
        P(None, None, "lat", "lon"),
        P("lat", "lon"),
        P("lat", "lon"),
        P("lat", "lon"),
    )
    return jax.shard_map(
        functools.partial(shards, mesh.shape["lat"], mesh.shape["lon"]),
        mesh=mesh,
        in_specs=placed,
        out_specs=(P(None, None, "lat", "lon"), P(None, None, "lat", "lon"), P("lat", "lon")),
        check_vma=False,
    )
```
